32 devices in a mesh: dom: 8 (over z, y), rep: 4 (over x, core).
Axes of the slice: x: 2, y: 2, z: 4, core: 2. Of those that a mesh axis runs over, the one named last changes fastest.
Arguments:
- feats: bfloat16 [256, 32768], P('rep', 'dom'), may hold values from -6 to 6
- w_self: bfloat16 [256, 256], P(None, 'rep'), may hold values from -0.375 to 0.375
- w_neigh: bfloat16 [256, 256], P(None, 'rep'), may hold values from -3 to 3
- local_cols: int32 [256, 2], P('dom'), may hold values from 0 to 31
- local_tiles: bfloat16 [256, 2, 128, 128], P('dom'), may hold values from 0 to 3, as said below
- send_list: int32 [8, 8, 2], P('dom'), may hold values from 0 to 31
- remote_rows: int32 [8, 8, 2], P('dom'), may hold values from 0 to 31
- remote_tiles: bfloat16 [8, 8, 2, 128, 128], P('dom'), may hold values from 0 to 3, as said below
- cotangent: bfloat16 [256, 32768], P('rep', 'dom'), may hold values from -6 to 6
Outputs:
- output: bfloat16 [256, 32768], P('rep', 'dom')
- grad_feats: bfloat16 [256, 32768], P('rep', 'dom')
- grad_w_self: float32 [256, 256], P(None, 'rep')
- grad_w_neigh: float32 [256, 256], P(None, 'rep')
The draws below stay inside these ranges and needn't reach their ends.
Inputs may be any that keep to these rules, and one draw needn't show every extreme that they name: `local_tiles`: edge weights: zero where a tile has no edge, positive otherwise. `remote_tiles`: edge weights: zero where a tile has no edge, positive otherwise.
All inputs are finite; a program needn't handle non-finite values.
Results may differ from the reference program's by a relative error of at most 0.0055.
Values may be sent and summed in bfloat16 or wider, within the bound.
A program may use at most 128 MiB of HBM per device.

```python
import math
import jax
import jax.numpy as jnp
from jax import lax

FEAT = 256
TILE = 128
BLK_DEV = 32
LOC = 2
SLOTS = 2
NODES = 32768
N_DOM = 8


def edge_weights(key, shape, density, low_scale):
    keep_key, value_key, scale_key = jax.random.split(key, 3)
    present = (jax.random.uniform(keep_key, shape, dtype=jnp.float32) < density).astype(jnp.float32)
    values = jax.random.uniform(value_key, shape, dtype=jnp.float32, minval=0.25, maxval=1.0)
    row_shape = tuple(shape[:-1]) + (1,)
    row_scale = jnp.exp(jax.random.uniform(scale_key, row_shape, dtype=jnp.float32, minval=math.log(low_scale), maxval=math.log(3.0)))
    return (present * values * row_scale).astype(jnp.bfloat16)


def draw_local_tiles(key, part):
    shape = (NODES // TILE, LOC, TILE, TILE)
    return edge_weights(jax.random.fold_in(key, 11), shape, 0.2, 0.3)


def draw_remote_tiles(key, part):
    shape = (N_DOM, N_DOM, SLOTS, TILE, TILE)
    return edge_weights(jax.random.fold_in(key, 23), shape, 0.2, 0.3)


def plant(result, own_key, least, largest):
    place = [jax.random.randint(jax.random.fold_in(own_key, axis), (), 0, length) for axis, length in enumerate(result.shape)]
    longest = result.shape.index(max(result.shape))
    next_to = place[:longest] + [(place[longest] + 1) % result.shape[longest]] + place[longest + 1:]
    return result.at[tuple(place)].set(least).at[tuple(next_to)].set(largest)


def level_of(key, shape, cuts, least, top_value):
    loudness = 1.0
    for dim, blocks in cuts:
        heights = jax.random.uniform(jax.random.fold_in(jax.random.fold_in(key, 6), dim), (blocks,), jnp.float32, least / len(cuts), top_value / len(cuts))
        loudness = loudness * jnp.repeat(jnp.exp(heights), shape[dim] // blocks).reshape((-1,) + (1,) * (len(shape) - 1 - dim))
    return loudness


def centred(own_key, shape, width, limit, shards=(), kind=jnp.bfloat16):
    gain = level_of(own_key, shape, shards, -0.22, 0.18) if shards else 1.0
    values = jax.random.normal(own_key, shape, jnp.float32) * width * gain
    return jnp.minimum(jnp.maximum(values, -limit), limit).astype(kind)


def setup_inputs(seed: int = 0) -> dict:
    splits = jax.random.split(jax.random.key(seed), 10)
    feats = centred(splits[0], (FEAT, NODES), 1.0, 6.0, ((0, 4), (1, 8)))
    w_self = centred(splits[1], (FEAT, FEAT), FEAT ** -0.5, 0.375, ((1, 4),))
    w_neigh = centred(splits[2], (FEAT, FEAT), (max(FEAT // 64, 1)) ** -0.5, 3.0, ((1, 4),))
    local_cols = plant(jax.random.randint(splits[3], (NODES // TILE, LOC), 0, BLK_DEV), jax.random.fold_in(splits[3], 1), 0, BLK_DEV - 1).astype(jnp.int32)
    local_tiles = draw_local_tiles(jax.random.fold_in(splits[9], 71), 0)
    send_list = plant(jax.random.randint(splits[5], (N_DOM, N_DOM, SLOTS), 0, BLK_DEV), jax.random.fold_in(splits[5], 1), 0, BLK_DEV - 1).astype(jnp.int32)
    remote_rows = plant(jax.random.randint(splits[6], (N_DOM, N_DOM, SLOTS), 0, BLK_DEV), jax.random.fold_in(splits[6], 1), 0, BLK_DEV - 1).astype(jnp.int32)
    remote_tiles = draw_remote_tiles(jax.random.fold_in(splits[9], 71), 0)
    cotangent = centred(splits[8], (FEAT, NODES), 1.0, 6.0, ((0, 4), (1, 8)))
    return dict(feats=feats, w_self=w_self, w_neigh=w_neigh, local_cols=local_cols, local_tiles=local_tiles, send_list=send_list, remote_rows=remote_rows, remote_tiles=remote_tiles, cotangent=cotangent)


def reference(feats, w_self, w_neigh, local_cols, local_tiles, send_list, remote_rows, remote_tiles, cotangent):
    highest = lax.Precision.HIGHEST
    feat_width, node_count = feats.shape
    block_total = node_count // TILE
    blocked = feats.reshape(feat_width, block_total, TILE)
    block_ids = jnp.arange(BLK_DEV, dtype=jnp.int32)
    local_view = local_tiles.reshape(N_DOM, BLK_DEV, LOC, TILE, TILE)
    col_view = local_cols.reshape(N_DOM, BLK_DEV, LOC)
    sender_base = (jnp.arange(N_DOM, dtype=jnp.int32) * BLK_DEV)[:, None]

    def forward_part(part):
        near_tiles = local_view[part].astype(jnp.float32)
        near_cols = (col_view[part] + part * BLK_DEV).astype(jnp.int32)
        gathered = blocked[:, near_cols].astype(jnp.float32)
        summed = jnp.einsum("fblj,blij->fbi", gathered, near_tiles, precision=highest)
        far_tiles = remote_tiles[part].astype(jnp.float32)
        far_blocks = (sender_base + send_list[:, part, :]).astype(jnp.int32)
        incoming = blocked[:, far_blocks].astype(jnp.float32)
        far_terms = jnp.einsum("fskj,skij->fski", incoming, far_tiles, precision=highest)
        placing = (remote_rows[part][:, :, None] == block_ids).astype(jnp.float32)
        summed = summed + jnp.einsum("fski,skb->fbi", far_terms, placing, precision=highest)
        far_sums = jnp.sum(far_tiles, axis=3)
        divisor = 1.0 + jnp.sum(near_tiles, axis=(1, 3)) + jnp.einsum("ski,skb->bi", far_sums, placing, precision=highest)
        return (summed / divisor).astype(jnp.bfloat16), divisor

    aggregates, divisors = lax.map(forward_part, jnp.arange(N_DOM, dtype=jnp.int32))
    aggregate = aggregates.transpose(1, 0, 2, 3).reshape(feat_width, node_count)
    divisor = divisors.reshape(block_total, TILE)

    preact = jnp.dot(w_self.T, feats, preferred_element_type=jnp.float32)
    preact = preact + jnp.dot(w_neigh.T, aggregate, preferred_element_type=jnp.float32)
    sigmoid_val = jax.nn.sigmoid(preact)
    output = (preact * sigmoid_val).astype(jnp.bfloat16)
    slope = sigmoid_val * (1.0 + preact * (1.0 - sigmoid_val))
    grad_pre = (cotangent.astype(jnp.float32) * slope).astype(jnp.bfloat16)
    grad_w_self = jnp.dot(feats, grad_pre.T, preferred_element_type=jnp.float32)
    grad_w_neigh = jnp.dot(aggregate, grad_pre.T, preferred_element_type=jnp.float32)
    back_self = jnp.dot(w_self, grad_pre, preferred_element_type=jnp.float32)
    back_agg = jnp.dot(w_neigh, grad_pre, preferred_element_type=jnp.float32)
    scaled = (back_agg.reshape(feat_width, block_total, TILE) / divisor).astype(jnp.bfloat16)

    def backward_part(part):
        near_tiles = local_view[part].astype(jnp.float32)
        own_rows = lax.dynamic_slice_in_dim(scaled, (part * BLK_DEV).astype(jnp.int32), BLK_DEV, 1).astype(jnp.float32)
        near_back = jnp.einsum("fbi,blij->fblj", own_rows, near_tiles, precision=highest)
        landing = (col_view[part][:, :, None] == block_ids).astype(jnp.float32)
        collected = jnp.einsum("fblj,blc->fcj", near_back, landing, precision=highest)
        far_rows = (sender_base + remote_rows[:, part, :]).astype(jnp.int32)
        picked = scaled[:, far_rows].astype(jnp.float32)
        far_tiles = remote_tiles[:, part].astype(jnp.float32)
        far_back = jnp.einsum("fdki,dkij->fdkj", picked, far_tiles, precision=highest)
        homing = (send_list[part][:, :, None] == block_ids).astype(jnp.float32)
        return collected + jnp.einsum("fdkj,dkc->fcj", far_back, homing, precision=highest)

    edge_parts = lax.map(backward_part, jnp.arange(N_DOM, dtype=jnp.int32))
    edge_grads = edge_parts.transpose(1, 0, 2, 3).reshape(feat_width, node_count)
    grad_feats = (back_self + edge_grads).astype(jnp.bfloat16)
    return output, grad_feats, grad_w_self, grad_w_neigh
```

```python
import functools

import jax
import jax.numpy as jnp
from jax import lax
from jax.experimental import pallas as pl
from jax.experimental.pallas import tpu as pltpu
from jax.sharding import PartitionSpec as P

MESH = pl.DeviceIdType.MESH
F32 = jnp.float32
BF16 = jnp.bfloat16
CHUNKS = 4
ONES = 16
KEEP = 8
NT = (((1,), (1,)), ((), ()))


def mm(a, b):
    return jnp.dot(a, b, preferred_element_type=F32)


def mm_nt(a, b):
    return lax.dot_general(a, b, NT, preferred_element_type=F32)


def equal_one(x, y):
    gap = x - y
    return (1 - jnp.minimum(gap * gap, 1)).astype(F32)


def rcopy(src, dst, send, recv, dom, rep):
    return pltpu.make_async_remote_copy(
        src_ref=src,
        dst_ref=dst,
        send_sem=send,
        recv_sem=recv,
        device_id={"dom": dom, "rep": rep},
        device_id_type=MESH,
    )


def greet(devices):
    barrier = pltpu.get_barrier_semaphore()
    for dom, rep in devices:
        pl.semaphore_signal(
            barrier, inc=1, device_id={"dom": dom, "rep": rep}, device_id_type=MESH
        )
    pl.semaphore_wait(barrier, len(devices))


def main_kernel(
    D,
    R,
    feats,
    wts_in,
    wtn_in,
    cols,
    slist,
    rrows,
    ltiles_h,
    rtiles_h,
    cot_h,
    out_o,
    acc_o,
    back_o,
    final_o,
    ltiles,
    rtiles,
    cot,
    blocks_of,
    hsend,
    hrecv,
    summed,
    far,
    inv,
    wts,
    wtn,
    wb,
    xf,
    xa,
    own,
    psend,
    precv,
    gp,
    gw,
    gpart,
    red,
    scaled,
    ret,
    nearb,
    loc_sem,
    h_s,
    h_r,
    ws_s,
    ws_r,
    wn_s,
    wn_r,
    xf_s,
    xf_r,
    xa_s,
    xa_r,
    pp_s,
    pp_r,
    gx_s,
    gx_r,
    gc_s,
    gc_r,
    b_s,
    b_r,
    p_s,
    p_r,
    f_s,
    f_r,
):
    d, r = lax.axis_index("dom"), lax.axis_index("rep")
    G = R // 2
    c, g = lax.rem(r, 2), lax.div(r, 2)
    mate = g * 2 + 1 - c
    F, N = feats.shape
    B, L, T, _ = ltiles.shape
    K = slist.shape[0]
    CH = N // CHUNKS
    CB = B // CHUNKS

    def cross(q):
        return lax.rem(g + q, G) * 2 + c

    loads = [
        pltpu.make_async_copy(ltiles_h, ltiles, loc_sem.at[0]),
        pltpu.make_async_copy(rtiles_h, rtiles, loc_sem.at[1]),
        pltpu.make_async_copy(cot_h, cot, loc_sem.at[2]),
    ]
    for load in loads:
        load.start()
    for b in range(B):
        blocks_of[b] = feats[:, b * T : (b + 1) * T]
    greet(
        [
            (lax.rem(d + p, D), cross(q))
            for q in range(G)
            for p in range(D)
            if p or q
        ]
        + [(d, lax.rem(g + q, G) * 2 + 1 - c) for q in range(G)]
    )

    def halo(p):
        return rcopy(
            hsend.at[p], hrecv.at[p], h_s.at[p], h_r.at[p], lax.rem(d + p, D), r
        )

    def pick(p, dst):
        for k in range(K):
            dst[p, k] = blocks_of[slist[k, lax.rem(d + p, D)]]

    def send_halo(p, carry):
        pick(p, hsend)
        halo(p).start()
        return carry

    lax.fori_loop(1, D, send_halo, 0)
    pick(0, hrecv)
    weight_copies, cross_weights = [], []
    sets = ((wts_in, wts, ws_s, ws_r), (wtn_in, wtn, wn_s, wn_r))
    chip = pl.ds(pl.multiple_of(g * 2 * F, 2 * F), 2 * F)
    for q in range(1, G):
        there = lax.rem(g + q, G)
        cut = pl.ds(pl.multiple_of(there * 2 * F, 2 * F), 2 * F)
        for src, dst, ss, rs in sets:
            cross_weights.append(
                rcopy(src.at[:, cut], dst.at[r], ss.at[q], rs.at[q], d, cross(q))
            )
    for src, dst, ss, rs in sets:
        weight_copies.append(
            rcopy(src.at[:, chip], dst.at[r], ss.at[0], rs.at[0], d, mate)
        )
    for copy in cross_weights + weight_copies:
        copy.start()
    feat_copy = rcopy(feats, xf.at[c], xf_s, xf_r, d, mate)
    feat_copy.start()
    wts[r] = wts_in[:, chip]
    wtn[r] = wtn_in[:, chip]
    xf[c] = feats[...]

    ones = jnp.ones((ONES, T), BF16)
    ones_wide = jnp.ones((ONES, L * T), BF16)
    loads[0].wait()

    def near(b, carry):
        left = jnp.concatenate(
            [
                blocks_of[cols[l, b]]
                for l in range(L)
            ],
            axis=1,
        )
        left = jnp.concatenate([left, ones_wide], axis=0)
        right = jnp.concatenate([ltiles[b, l] for l in range(L)], axis=1)
        summed[b] = mm_nt(left, right)[: F + KEEP]
        return carry

    lax.fori_loop(0, B, near, 0, unroll=4)
    for copy in cross_weights:
        copy.wait_recv()
    for q in range(1, G):
        t = lax.rem(g - q + G, G) * 2 + c
        for _, dst, ss, rs in sets:
            slot = G + q - 1
            copy = rcopy(dst.at[t], dst.at[t], ss.at[slot], rs.at[slot], d, mate)
            copy.start()
            weight_copies.append(copy)
    loads[1].wait()

    def far_step(p, carry):
        source = lax.rem(d - p + D, D)
        for k in range(K):
            left = jnp.concatenate([hrecv[p, k], ones], axis=0)
            far[p * K + k] = mm_nt(left, rtiles[source, k])[: F + KEEP]
        return carry

    def far_wait(p, carry):
        halo(p).wait_recv()
        return carry

    far_step(0, 0)
    lax.fori_loop(1, D, far_wait, 0)
    lax.fori_loop(1, D, far_step, 0, unroll=7)

    agg_copies = []
    for ch in range(CHUNKS):

        def place(i, carry):
            b = ch * CB + i
            total = summed[b]

            def add(p, total):
                source = lax.rem(d - p + D, D)
                for k in range(K):
                    hit = equal_one(rrows[k, source], b)
                    total = total + far[p * K + k] * hit
                return total

            total = lax.fori_loop(0, D, add, total, unroll=8)
            inverse = 1.0 / (1.0 + total[F:])
            at = pl.multiple_of(i * T, T)
            whole_at = pl.multiple_of(b * T, T)
            inv[:, pl.ds(whole_at, T)] = inverse
            xa[ch, c, :, pl.ds(at, T)] = (total[:F] * inverse[:1]).astype(BF16)
            return carry

        lax.fori_loop(0, CB, place, 0)
        copy = rcopy(xa.at[ch, c], xa.at[ch, c], xa_s.at[ch], xa_r.at[ch], d, mate)
        copy.start()
        agg_copies.append(copy)

    for copy in weight_copies:
        copy.wait_recv()
    for i, ref in enumerate((wts, wtn)):
        block = ref[...].reshape(R * F, 2 * F)
        turned = block.astype(F32).T.astype(BF16)
        wb[i] = turned.reshape(2, F, R * F)
    lefts = []
    for q in range(G):
        t = cross(q)
        lefts.append(jnp.concatenate([wts[t], wtn[t]], axis=1))
    left = jnp.concatenate(lefts, axis=0)
    feat_copy.wait_recv()

    def stacked(ch):
        near_part = xf[:, :, ch * CH : (ch + 1) * CH].reshape(2 * F, CH)
        return jnp.concatenate([near_part, xa[ch].reshape(2 * F, CH)], axis=0)

    part_copies = []
    for ch in range(CHUNKS):
        agg_copies[ch].wait_recv()
        part = mm(left, stacked(ch))
        for q in range(1, G):
            psend[q, ch] = part[q * F : (q + 1) * F].astype(BF16)
            copy = rcopy(
                psend.at[q, ch],
                precv.at[q, ch],
                pp_s.at[q, ch],
                pp_r.at[q, ch],
                d,
                cross(q),
            )
            copy.start()
            part_copies.append(copy)
        own[ch] = part[:F]

    loads[2].wait()
    cross_copies, mate_copies = [], []
    for ch in range(CHUNKS):
        preact = own[ch]
        for q in range(1, G):
            part_copies[ch * (G - 1) + q - 1].wait_recv()
            preact = preact + precv[q, ch].astype(F32)
        s = jax.nn.sigmoid(preact)
        at = slice(ch * CH, (ch + 1) * CH)
        out_o[:, at] = (preact * s).astype(BF16)
        slope = s * (1.0 + preact * (1.0 - s))
        gp[ch, r] = (cot[:, at].astype(F32) * slope).astype(BF16)
        for q in range(1, G):
            copy = rcopy(
                gp.at[ch, r],
                gp.at[ch, r],
                gx_s.at[q, ch],
                gx_r.at[q, ch],
                d,
                cross(q),
            )
            copy.start()
            cross_copies.append(copy)
        copy = rcopy(
            gp.at[ch, r], gp.at[ch, r], gc_s.at[0, ch], gc_r.at[0, ch], d, mate
        )
        copy.start()
        mate_copies.append(copy)

    back_left = jnp.concatenate([wb[0, c], wb[1, c]], axis=0)

    def back_chunk(ch):
        later = CHUNKS + ch * (G - 1)
        for copy in [mate_copies[ch]] + mate_copies[later : later + G - 1]:
            copy.wait_recv()
        back = mm(back_left, gp[ch].reshape(R * F, CH))
        for i in range(CB):
            b = ch * CB + i
            at = slice(i * T, (i + 1) * T)
            whole_at = slice(b * T, (b + 1) * T)
            acc_o[:, whole_at] = back[:F, at]
            scaled[b] = (back[F:, at] * inv[:1, whole_at]).astype(BF16)

    def scatter_all():
        def near_back(b, carry):
            right = jnp.concatenate([ltiles[b, l] for l in range(L)], axis=1)
            both = mm(scaled[b], right)
            for l in range(L):
                nearb[l, b] = both[:, l * T : (l + 1) * T]
            return carry

        lax.fori_loop(0, B, near_back, 0, unroll=4)

        def gather_back(block, carry):
            at = pl.ds(pl.multiple_of(block * T, T), T)

            def add(i, total):
                for l in range(L):
                    total = total + nearb[l, i] * equal_one(cols[l, i], block)
                return total

            acc_o[:, at] = lax.fori_loop(0, B, add, acc_o[:, at], unroll=8)
            return carry

        lax.fori_loop(0, B, gather_back, 0)

    grads = jnp.zeros((G * F, 4 * F), F32)
    for ch in range(CHUNKS):
        blocks = [gp[ch, r]]
        for q in range(1, G):
            cross_copies[ch * (G - 1) + q - 1].wait_recv()
            t = lax.rem(g - q + G, G) * 2 + c
            copy = rcopy(
                gp.at[ch, t], gp.at[ch, t], gc_s.at[q, ch], gc_r.at[q, ch], d, mate
            )
            copy.start()
            mate_copies.append(copy)
        for q in range(1, G):
            blocks.append(gp[ch, cross(q)])
        grads = grads + mm_nt(jnp.concatenate(blocks, axis=0), stacked(ch))
        if ch >= 1:
            back_chunk(ch - 1)
    rows = gw.shape[2]
    for p in range(D):
        for q in range(G):
            gw[p, q] = grads[q * F + p * rows : q * F + (p + 1) * rows]

    def piece(p):
        to = lax.rem(d + p, D)
        return rcopy(gw.at[to], gpart.at[p], p_s.at[p], p_r.at[p], to, r)

    def send_piece(p, carry):
        piece(p).start()
        return carry

    lax.fori_loop(1, D, send_piece, 0)

    back_chunk(CHUNKS - 1)

    def away(p, dst, slot):
        source = lax.rem(d + p, D)
        for k in range(K):
            block = scaled[rrows[k, source]]
            dst[slot, k] = mm(block, rtiles[source, k]).astype(BF16)

    def returned(p):
        to = lax.rem(d + p, D)
        return rcopy(ret.at[p], back_o.at[d], b_s.at[p], b_r.at[p], to, r)

    def send_back(p, carry):
        away(p, ret, p)
        returned(p).start()
        return carry

    lax.fori_loop(1, D, send_back, 0, unroll=7)
    away(0, back_o, d)

    def take_piece(p, total):
        piece(p).wait_recv()
        return total + gpart[p]

    red[...] = lax.fori_loop(1, D, take_piece, gw[d])
    finals = []
    for q in range(G):
        for p in range(D):
            if p or q:
                copy = rcopy(
                    red.at[q],
                    final_o.at[g, d],
                    f_s.at[q, p],
                    f_r.at[q, p],
                    lax.rem(d + p, D),
                    cross(q),
                )
                copy.start()
                finals.append(copy)
    final_o[g, d] = red[0]

    scatter_all()

    def finish_back(p, carry):
        returned(p).wait()
        piece(p).wait_send()
        return carry

    lax.fori_loop(1, D, finish_back, 0)
    for copy in finals:
        copy.wait_recv()

    def drain(p, carry):
        halo(p).wait_send()
        return carry

    lax.fori_loop(1, D, drain, 0)
    for copy in (
        weight_copies
        + cross_weights
        + [feat_copy]
        + agg_copies
        + part_copies
        + cross_copies
        + mate_copies
        + finals
    ):
        copy.wait_send()


def finish_kernel(
    slist, acc, back, final, out_v, out_o, gf_o, gs_o, gn_o, total, sem
):
    store = pltpu.make_async_copy(out_v, out_o, sem)
    store.start()
    total[...] = acc[...]
    D, K, _, T = back.shape
    G, _, rows, width = final.shape
    half = width // 2

    def home(s, carry):
        for k in range(K):
            at = pl.ds(pl.multiple_of(slist[k, s] * T, T), T)
            total[:, at] = total[:, at] + back[s, k].astype(F32)
        return carry

    lax.fori_loop(0, D, home, 0)
    gf_o[...] = total[...].astype(BF16)
    for h in range(G):
        at = slice(h * half, (h + 1) * half)
        for p in range(D):
            part = final[h, p]
            where = slice(p * rows, (p + 1) * rows)
            gs_o[where, at] = part[:, :half]
            gn_o[where, at] = part[:, half:]
    store.wait()


def local(
    D,
    R,
    feats,
    w_self,
    w_neigh,
    local_cols,
    local_tiles,
    send_list,
    remote_rows,
    remote_tiles,
    cotangent,
):
    F, N = feats.shape
    B, L, T, _ = local_tiles.shape
    K = send_list.shape[2]
    G = R // 2
    CH = N // CHUNKS
    rows = F // D
    vmem = pl.BlockSpec(memory_space=pltpu.VMEM)
    smem = pl.BlockSpec(memory_space=pltpu.SMEM)
    hbm = pl.BlockSpec(memory_space=pltpu.HBM)
    dma = pltpu.SemaphoreType.DMA
    slist = jnp.swapaxes(send_list, 1, 2)[0]
    rrows = jnp.swapaxes(remote_rows, 1, 2)[0]
    far_tiles = remote_tiles[0]
    limit = 56 * 1024 * 1024
    output, acc, back, final = pl.pallas_call(
        functools.partial(main_kernel, D, R),
        out_shape=(
            pltpu.VMEM((F, N), BF16),
            pltpu.VMEM((F, N), F32),
            pltpu.VMEM((D, K, F, T), BF16),
            pltpu.VMEM((G, D, rows, 4 * F), F32),
        ),
        in_specs=[vmem, vmem, vmem, smem, smem, smem, hbm, hbm, hbm],
        out_specs=(vmem, vmem, vmem, vmem),
        scratch_shapes=[
            pltpu.VMEM((B, L, T, T), BF16),
            pltpu.VMEM((D, K, T, T), BF16),
            pltpu.VMEM((F, N), BF16),
            pltpu.VMEM((B, F, T), BF16),
            pltpu.VMEM((D, K, F, T), BF16),
            pltpu.VMEM((D, K, F, T), BF16),
            pltpu.VMEM((B, F + KEEP, T), F32),
            pltpu.VMEM((D * K, F + KEEP, T), F32),
            pltpu.VMEM((KEEP, N), F32),
            pltpu.VMEM((R, F, 2 * F), BF16),
            pltpu.VMEM((R, F, 2 * F), BF16),
            pltpu.VMEM((2, 2, F, R * F), BF16),
            pltpu.VMEM((2, F, N), BF16),
            pltpu.VMEM((CHUNKS, 2, F, CH), BF16),
            pltpu.VMEM((CHUNKS, F, CH), F32),
            pltpu.VMEM((G, CHUNKS, F, CH), BF16),
            pltpu.VMEM((G, CHUNKS, F, CH), BF16),
            pltpu.VMEM((CHUNKS, R, F, CH), BF16),
            pltpu.VMEM((D, G, rows, 4 * F), F32),
            pltpu.VMEM((D, G, rows, 4 * F), F32),
            pltpu.VMEM((G, rows, 4 * F), F32),
            pltpu.VMEM((B, F, T), BF16),
            pltpu.VMEM((D, K, F, T), BF16),
            pltpu.VMEM((L, B, F, T), F32),
            dma((3,)),
            dma((D,)),
            dma((D,)),
            dma((R,)),
            dma((R,)),
            dma((R,)),
            dma((R,)),
            dma,
            dma,
            dma((CHUNKS,)),
            dma((CHUNKS,)),
            dma((G, CHUNKS)),
            dma((G, CHUNKS)),
            dma((G, CHUNKS)),
            dma((G, CHUNKS)),
            dma((G, CHUNKS)),
            dma((G, CHUNKS)),
            dma((D,)),
            dma((D,)),
            dma((D,)),
            dma((D,)),
            dma((G, D)),
            dma((G, D)),
        ],
        compiler_params=pltpu.CompilerParams(
            collective_id=0, has_side_effects=True, vmem_limit_bytes=limit
        ),
        name="layer_main",
    )(
        feats,
        w_self.T,
        w_neigh.T,
        local_cols.T,
        slist,
        rrows,
        local_tiles,
        far_tiles,
        cotangent,
    )
    output, grad_feats, gs, gn = pl.pallas_call(
        finish_kernel,
        out_shape=(
            jax.ShapeDtypeStruct((F, N), BF16),
            jax.ShapeDtypeStruct((F, N), BF16),
            jax.ShapeDtypeStruct((F, R * F), F32),
            jax.ShapeDtypeStruct((F, R * F), F32),
        ),
        in_specs=[smem, vmem, vmem, vmem, vmem],
        out_specs=(hbm, vmem, vmem, vmem),
        scratch_shapes=[pltpu.VMEM((F, N), F32), dma],
        compiler_params=pltpu.CompilerParams(vmem_limit_bytes=24 * 1024 * 1024),
        name="finish",
    )(slist, acc, back, final, output)
    return output, grad_feats, gs.T, gn.T


def solution(mesh):
    placed = (
        P("rep", "dom"),
        P(None, "rep"),
        P(None, "rep"),
        P("dom", None),
        P("dom", None, None, None),
        P("dom", None, None),
        P("dom", None, None),
        P("dom", None, None, None, None),
        P("rep", "dom"),
    )
    return jax.shard_map(
        functools.partial(local, mesh.shape["dom"], mesh.shape["rep"]),
        mesh=mesh,
        in_specs=placed,
        out_specs=(P("rep", "dom"), P("rep", "dom"), P(None, "rep"), P(None, "rep")),
        check_vma=False,
    )
```

```python
import functools

import jax
import jax.numpy as jnp
from jax import lax
from jax.experimental import pallas as pl
from jax.experimental.pallas import tpu as pltpu
from jax.sharding import PartitionSpec as P

MESH = pl.DeviceIdType.MESH
F32 = jnp.float32
BF16 = jnp.bfloat16
CHUNKS = 4
PIECES = 4
ONES = 16
KEEP = 8
NT = (((1,), (1,)), ((), ()))


def mm(a, b):
    return jnp.dot(a, b, preferred_element_type=F32)


def mm_nt(a, b):
    return lax.dot_general(a, b, NT, preferred_element_type=F32)


def equal_int(x, y):
    gap = x - y
    return 1 - jnp.minimum(gap * gap, 1)


def equal_one(x, y):
    return equal_int(x, y).astype(F32)


def rcopy(src, dst, send, recv, dom, rep):
    return pltpu.make_async_remote_copy(
        src_ref=src,
        dst_ref=dst,
        send_sem=send,
        recv_sem=recv,
        device_id={"dom": dom, "rep": rep},
        device_id_type=MESH,
    )


def main_kernel(
    D,
    R,
    feats_h,
    wts_h,
    wtn_h,
    cols,
    slist,
    rrows,
    ltiles_h,
    rtiles_h,
    cot_h,
    out_o,
    acc_o,
    back_o,
    final_o,
    fown,
    fmir,
    xchip,
    xmir,
    ltiles,
    rtiles,
    wall,
    wl,
    wb,
    cotb,
    hsend,
    hx,
    sums,
    chain,
    inv,
    xa,
    pre,
    gpb,
    outm,
    accm,
    scaled,
    scm,
    gmate,
    gin,
    gw,
    gpart,
    red,
    ret,
    nearb,
    prev,
    last,
    f_l,
    own_l,
    mir_l,
    w_l,
    c_l,
    t_l,
    xs_s,
    xs_r,
    xm_s,
    xm_r,
    xf_s,
    xf_r,
    h_s,
    h_r,
    hf_s,
    hf_r,
    w_s,
    w_r,
    cm_s,
    cm_r,
    cx_s,
    cx_r,
    om_s,
    om_r,
    am_s,
    am_r,
    sm_s,
    sm_r,
    gm_s,
    gm_r,
    b_s,
    b_r,
    p_s,
    p_r,
    f_s,
    f_r,
):
    d, r = lax.axis_index("dom"), lax.axis_index("rep")
    G = R // 2
    c, g = lax.rem(r, 2), lax.div(r, 2)
    mate = g * 2 + 1 - c
    F, N = feats_h.shape
    B, L, T, _ = ltiles.shape
    K = slist.shape[0]
    RF, CF, S = R * F, 2 * F, D * K
    BH, NH = B // 2, N // 2
    CB = BH // CHUNKS
    CH = CB * T
    PB = B // PIECES
    chips = [lax.rem(g + q, G) for q in range(G)]

    def peer(q, core):
        return chips[q] * 2 + core

    def ahead(p):
        return lax.rem(d + p, D)

    barrier = pltpu.get_barrier_semaphore()
    greeted = [(ahead(p), r) for p in range(1, D)] + [(d, mate)]
    greeted += [(d, peer(q, core)) for q in range(1, G) for core in range(2)]
    for dom, rep in greeted:
        pl.semaphore_signal(
            barrier, inc=1, device_id={"dom": dom, "rep": rep}, device_id_type=MESH
        )
    feat_loads = [
        pltpu.make_async_copy(
            feats_h.at[:, b * T : (b + 1) * T], fown.at[b], f_l.at[b]
        )
        for b in range(B)
    ]
    weight_loads = [
        pltpu.make_async_copy(src, wall.at[r, i], w_l.at[i])
        for i, src in enumerate((wts_h, wtn_h))
    ]

    def half_cut(core, ch):
        return pl.ds(pl.multiple_of(core * NH + ch * CH, T), CH)

    cot_loads = [
        pltpu.make_async_copy(cot_h.at[:, half_cut(c, ch)], cotb.at[ch, r], c_l.at[ch])
        for ch in range(CHUNKS)
    ]
    tile_loads = [
        pltpu.make_async_copy(ltiles_h, ltiles, t_l.at[0]),
        pltpu.make_async_copy(rtiles_h, rtiles, t_l.at[1]),
    ]
    for load in feat_loads + weight_loads + tile_loads + cot_loads:
        load.start()

    def previous(s, carry):
        row = rrows[lax.rem(s, K), lax.rem(d - lax.div(s, K) + D, D)]

        def look(j, found):
            other = rrows[lax.rem(j, K), lax.rem(d - lax.div(j, K) + D, D)]
            return jnp.maximum(found, (j + 1) * equal_int(row, other))

        prev[s] = lax.fori_loop(0, s, look, 0)
        return carry

    lax.fori_loop(0, S, previous, 0)

    def latest(i, carry):
        def look(j, found):
            other = rrows[lax.rem(j, K), lax.rem(d - lax.div(j, K) + D, D)]
            return jnp.maximum(found, (j + 1) * equal_int(c * BH + i, other))

        last[i] = lax.fori_loop(0, S, look, 0)
        return carry

    lax.fori_loop(0, BH, latest, 0)
    for q in range(G):
        chain[q, 0] = jnp.zeros((CF + KEEP, T), F32)
    for load in feat_loads:
        load.wait()
    pl.semaphore_wait(barrier, len(greeted))

    sends = []

    def go(copy):
        copy.start()
        sends.append(copy)
        return copy

    def piece_cut(j):
        return pl.ds(j * PB, PB)

    cross_feats = [
        [
            go(
                rcopy(
                    fown.at[piece_cut(j)],
                    fmir.at[G - q - 1, piece_cut(j)],
                    xs_s.at[q, j],
                    xs_r.at[G - q, j],
                    d,
                    peer(q, c),
                )
            )
            for q in range(1, G)
        ]
        for j in range(PIECES)
    ]
    mate_feat = go(rcopy(fown, xchip.at[c], xm_s, xm_r, d, mate))

    def halo(q, p):
        return rcopy(
            hsend.at[q, p], hx.at[q, c, p], h_s.at[q, p], h_r.at[q, p], ahead(p), r
        )

    def halo_on(q, p):
        return rcopy(
            hx.at[q, c, p], hx.at[q, c, p], hf_s.at[q, p], hf_r.at[q, p], d, mate
        )

    def send_halo(p, carry):
        for k in range(K):
            hsend[0, p, k] = fown[slist[k, ahead(p)]]
        halo(0, p).start()
        return carry

    lax.fori_loop(1, D, send_halo, 0)
    own_copy = pltpu.make_async_copy(fown, xchip.at[c], own_l)
    own_copy.start()
    for load in weight_loads:
        load.wait()
    mate_weights = go(rcopy(wall.at[r], wall.at[r], w_s.at[0], w_r.at[0], d, mate))
    cross_weights = [
        go(rcopy(wall.at[r], wall.at[r], w_s.at[q], w_r.at[q], d, peer(q, c)))
        for q in range(1, G)
    ]
    mate_cots = []
    for ch in range(CHUNKS):
        for q in range(1, G):
            for core in range(2):
                go(
                    rcopy(
                        cot_h.at[:, half_cut(core, ch)],
                        cotb.at[ch, r],
                        cx_s.at[q, core, ch],
                        cx_r.at[q, c, ch],
                        d,
                        peer(q, core),
                    )
                )
        mate_cots.append(
            go(
                rcopy(
                    cot_h.at[:, half_cut(1 - c, ch)],
                    cotb.at[ch, r],
                    cm_s.at[ch],
                    cm_r.at[ch],
                    d,
                    mate,
                )
            )
        )

    def wait_cot(ch):
        cot_loads[ch].wait()
        mate_cots[ch].wait_recv()
        for q in range(1, G):
            for core in range(2):
                slot = cotb.at[ch, r]
                copy = rcopy(
                    slot, slot, cx_s.at[q, core, ch], cx_r.at[q, core, ch], d, mate
                )
                copy.wait_recv()

    ones = jnp.ones((ONES, T), BF16)
    ones_wide = jnp.ones((ONES, L * T), BF16)

    def near(q, x):
        def step(i, carry):
            b = c * BH + i
            left = jnp.concatenate(
                [
                    jnp.concatenate([x(core, cols[l, b]) for core in range(2)], axis=0)
                    for l in range(L)
                ],
                axis=1,
            )
            if q == 0:
                left = jnp.concatenate([left, ones_wide], axis=0)
            right = jnp.concatenate([ltiles[b, l] for l in range(L)], axis=1)
            high = CF + KEEP if q == 0 else CF
            sums[q, i, :high] = mm_nt(left, right)[:high]
            return carry

        lax.fori_loop(0, BH, step, 0, unroll=4)

    def far(q):
        def step(p, carry):
            source = lax.rem(d - p + D, D)
            high = CF + KEEP if q == 0 else CF
            for k in range(K):
                s = p * K + k
                left = [hx[q, core, p, k] for core in range(2)]
                if q == 0:
                    left.append(ones)
                term = mm_nt(jnp.concatenate(left, axis=0), rtiles[source, k])[:high]
                chain[q, s + 1, :high] = term + chain[q, prev[s], :high]
            return carry

        lax.fori_loop(0, D, step, 0, unroll=4)

    def place(q):
        def step(i, carry):
            if q == 0:
                total = sums[q, i] + chain[q, last[i]]
                inverse = 1.0 / (1.0 + total[CF:])
                inv[i] = inverse
            else:
                total = sums[q, i, :CF] + chain[q, last[i], :CF]
                inverse = inv[i]
            xa[q, i] = (total[:CF] * inverse[:1]).astype(BF16)
            return carry

        lax.fori_loop(0, BH, step, 0, unroll=4)

    feats_on = []

    def pass_feats(j):
        for q in range(1, G):
            cross_feats[j][G - q - 1].wait_recv()
            feats_on.append(
                go(
                    rcopy(
                        fmir.at[q - 1, piece_cut(j)],
                        xmir.at[q - 1, c, piece_cut(j)],
                        xf_s.at[q, j],
                        xf_r.at[q, j],
                        d,
                        mate,
                    )
                )
            )

    def pass_halo(q):
        def step(p, carry):
            halo(q, p).wait_recv()
            halo_on(q, p).start()
            return carry

        lax.fori_loop(1, D, step, 0)

    def wait_halo(q):
        def step(p, carry):
            halo_on(q, p).wait_recv()
            return carry

        lax.fori_loop(1, D, step, 0)

    own_copy.wait()
    mate_feat.wait_recv()
    for k in range(K):
        for core in range(2):
            hx[0, core, 0, k] = xchip[core, slist[k, d]]
    tile_loads[0].wait()
    near(0, lambda core, col: xchip[core, col])
    tile_loads[1].wait()
    pass_feats(0)
    pass_halo(0)
    for j in range(1, PIECES - 1):
        pass_feats(j)
    wait_halo(0)
    far(0)
    place(0)
    pass_feats(PIECES - 1)
    mirror_copies = [
        pltpu.make_async_copy(fmir.at[q - 1], xmir.at[q - 1, c], mir_l.at[q - 1])
        for q in range(1, G)
    ]

    for q in range(1, G):

        def send_mirror(p, carry):
            for k in range(K):
                hsend[q, p, k] = fmir[q - 1, slist[k, ahead(p)]]
            halo(q, p).start()
            return carry

        lax.fori_loop(1, D, send_mirror, 0)
    for copy in mirror_copies:
        copy.start()
    weights_on = []
    for q in range(1, G):
        t = lax.rem(g - q + G, G) * 2 + c
        cross_weights[q - 1].wait_recv()
        slot = G + q - 1
        weights_on.append(
            go(rcopy(wall.at[t], wall.at[t], w_s.at[slot], w_r.at[slot], d, mate))
        )
    mate_weights.wait_recv()
    for copy in weights_on:
        copy.wait_recv()
    order = [r, mate] + [
        rep for q in range(1, G) for rep in (peer(q, c), peer(q, 1 - c))
    ]
    for i in range(2):
        for n, t in enumerate(order):
            for q in range(G):
                cut = pl.ds(pl.multiple_of(chips[q] * CF, CF), CF)
                wl[i, n * F : (n + 1) * F, q * CF : (q + 1) * CF] = wall[t, i, :, cut]
        turned = wl[i, :, :CF].astype(F32).T.astype(BF16)
        wb[i] = turned.reshape(2, F, RF)
    for copy in mirror_copies:
        copy.wait()
    for copy in feats_on:
        copy.wait_recv()
    for q in range(1, G):
        for k in range(K):
            for core in range(2):
                hx[q, core, 0, k] = xmir[q - 1, core, slist[k, d]]
        near(q, lambda core, col: xmir[q - 1, core, col])

    def stacked_x(ch):
        parts = []
        for i in range(CB):
            b = c * BH + ch * CB + i
            rows = [xchip[0, b], xchip[1, b]]
            for q in range(1, G):
                rows += [xmir[q - 1, 0, b], xmir[q - 1, 1, b]]
            parts.append(jnp.concatenate(rows, axis=0))
        return jnp.concatenate(parts, axis=1)

    def stacked_a(ch):
        return jnp.concatenate(
            [
                jnp.concatenate([xa[q, ch * CB + i] for q in range(G)], axis=0)
                for i in range(CB)
            ],
            axis=1,
        )

    for ch in range(CHUNKS):
        pre[ch] = mm(wl[0], stacked_x(ch))
    for q in range(1, G):
        pass_halo(q)
    for q in range(1, G):
        wait_halo(q)
        far(q)
        place(q)

    back_left = jnp.concatenate([wb[0, c], wb[0, 1 - c], wb[1, c], wb[1, 1 - c]], axis=0)
    grads = jnp.zeros((CF, 2 * RF), F32)
    out_copies, acc_copies, scaled_copies = [], [], []
    for ch in range(CHUNKS):
        cut = half_cut(c, ch)
        agg = stacked_a(ch)
        preact = pre[ch] + mm(wl[1], agg)
        s = jax.nn.sigmoid(preact)
        result = (preact[:CF] * s[:CF]).astype(BF16)
        out_o[:, cut] = result[:F]
        outm[ch] = result[F:]
        slope = s * (1.0 + preact * (1.0 - s))
        wait_cot(ch)
        cot = jnp.concatenate([cotb[ch, t] for t in order], axis=0)
        gp = (cot.astype(F32) * slope).astype(BF16)
        gpb[ch] = gp
        back = mm(back_left, gpb[ch])
        at = pl.ds(c * BH + ch * CB, CB)
        for i in range(CB):
            lane = slice(i * T, (i + 1) * T)
            inverse = inv[ch * CB + i][:1]
            scaled[c * BH + ch * CB + i] = (back[CF : CF + F, lane] * inverse).astype(
                BF16
            )
            scm[ch, i] = (back[CF + F :, lane] * inverse).astype(BF16)
        scaled_copies.append(
            go(rcopy(scm.at[ch], scaled.at[at], sm_s.at[ch], sm_r.at[ch], d, mate))
        )
        acc_o[:, cut] = back[:F]
        accm[ch] = back[F:CF]
        acc_copies.append(
            go(rcopy(accm.at[ch], acc_o.at[:, cut], am_s.at[ch], am_r.at[ch], d, mate))
        )
        out_copies.append(
            go(rcopy(outm.at[ch], out_o.at[:, cut], om_s.at[ch], om_r.at[ch], d, mate))
        )
        both = jnp.concatenate([stacked_x(ch), agg], axis=0)
        grads = grads + mm_nt(gpb[ch, :CF], both)
    gmate[...] = grads[F:]
    grad_copy = go(rcopy(gmate, gin, gm_s, gm_r, d, mate))

    for copy in scaled_copies:
        copy.wait_recv()

    def away(p, dst, slot):
        source = ahead(p)
        for k in range(K):
            block = scaled[rrows[k, source]]
            dst[slot, k] = mm(block, rtiles[source, k]).astype(BF16)

    def returned(p):
        return rcopy(ret.at[p], back_o.at[d], b_s.at[p], b_r.at[p], ahead(p), r)

    def send_back(p, carry):
        away(p, ret, p)
        returned(p).start()
        return carry

    lax.fori_loop(1, D, send_back, 0, unroll=7)
    away(0, back_o, d)

    rows = F // D
    grad_copy.wait_recv()
    own = grads[:F] + gin[...]
    for p in range(D):
        for i in range(2):
            for q in range(G):
                to = pl.ds(pl.multiple_of(i * RF + chips[q] * CF, CF), CF)
                lane = slice(i * RF + q * CF, i * RF + (q + 1) * CF)
                gw[p, :, to] = own[p * rows : (p + 1) * rows, lane]

    def piece(p):
        to = ahead(p)
        return rcopy(gw.at[to], gpart.at[p], p_s.at[p], p_r.at[p], to, r)

    def send_piece(p, carry):
        piece(p).start()
        return carry

    lax.fori_loop(1, D, send_piece, 0)

    def near_back(b, carry):
        right = jnp.concatenate([ltiles[b, l] for l in range(L)], axis=1)
        both = mm(scaled[b], right)
        for l in range(L):
            nearb[l, b] = both[:, l * T : (l + 1) * T]
        return carry

    lax.fori_loop(0, B, near_back, 0, unroll=4)
    for copy in acc_copies:
        copy.wait_recv()

    def gather_back(block, carry):
        at = pl.ds(pl.multiple_of(block * T, T), T)

        def add(i, total):
            for l in range(L):
                total = total + nearb[l, i] * equal_one(cols[l, i], block)
            return total

        acc_o[:, at] = lax.fori_loop(0, B, add, acc_o[:, at], unroll=8)
        return carry

    lax.fori_loop(0, BH, gather_back, 0)

    def take_piece(p, total):
        piece(p).wait_recv()
        return total + gpart[p]

    red[...] = lax.fori_loop(1, D, take_piece, gw[d])

    def final(p):
        return rcopy(red, final_o.at[d], f_s.at[p], f_r.at[p], ahead(p), r)

    def send_final(p, carry):
        final(p).start()
        return carry

    lax.fori_loop(1, D, send_final, 0)
    final_o[d] = red[...]
    lax.fori_loop(BH, B, gather_back, 0)
    for copy in out_copies:
        copy.wait_recv()

    def drain(p, carry):
        for q in range(G):
            halo(q, p).wait_send()
            halo_on(q, p).wait_send()
        returned(p).wait()
        piece(p).wait_send()
        final(p).wait()
        return carry

    lax.fori_loop(1, D, drain, 0)
    for copy in sends:
        copy.wait_send()


def finish_kernel(slist, acc, back, final, out_v, out_o, gf_o, gs_o, gn_o, total, sem):
    store = pltpu.make_async_copy(out_v, out_o, sem)
    store.start()
    total[...] = acc[...]
    D, K, _, T = back.shape
    _, rows, width = final.shape
    half = width // 2

    def home(s, carry):
        for k in range(K):
            at = pl.ds(pl.multiple_of(slist[k, s] * T, T), T)
            total[:, at] = total[:, at] + back[s, k].astype(F32)
        return carry

    lax.fori_loop(0, D, home, 0)
    gf_o[...] = total[...].astype(BF16)
    for p in range(D):
        part = final[p]
        where = slice(p * rows, (p + 1) * rows)
        gs_o[where, :] = part[:, :half]
        gn_o[where, :] = part[:, half:]
    store.wait()


def local(
    D,
    R,
    feats,
    w_self,
    w_neigh,
    local_cols,
    local_tiles,
    send_list,
    remote_rows,
    remote_tiles,
    cotangent,
):
    F, N = feats.shape
    B, L, T, _ = local_tiles.shape
    K = send_list.shape[2]
    G = R // 2
    RF, CF, S = R * F, 2 * F, D * K
    BH = B // 2
    CB = BH // CHUNKS
    CH = CB * T
    rows = F // D
    M = max(G - 1, 1)
    vmem = pl.BlockSpec(memory_space=pltpu.VMEM)
    smem = pl.BlockSpec(memory_space=pltpu.SMEM)
    hbm = pl.BlockSpec(memory_space=pltpu.HBM)
    dma = pltpu.SemaphoreType.DMA
    slist = jnp.swapaxes(send_list, 1, 2)[0]
    rrows = jnp.swapaxes(remote_rows, 1, 2)[0]
    far_tiles = remote_tiles[0]
    limit = 56 * 1024 * 1024
    output, acc, back, final = pl.pallas_call(
        functools.partial(main_kernel, D, R),
        out_shape=(
            pltpu.VMEM((F, N), BF16),
            pltpu.VMEM((F, N), F32),
            pltpu.VMEM((D, K, F, T), BF16),
            pltpu.VMEM((D, rows, 2 * RF), F32),
        ),
        in_specs=[hbm, hbm, hbm, smem, smem, smem, hbm, hbm, hbm],
        out_specs=(vmem, vmem, vmem, vmem),
        scratch_shapes=[
            pltpu.VMEM((B, F, T), BF16),
            pltpu.VMEM((M, B, F, T), BF16),
            pltpu.VMEM((2, B, F, T), BF16),
            pltpu.VMEM((M, 2, B, F, T), BF16),
            pltpu.VMEM((B, L, T, T), BF16),
            pltpu.VMEM((D, K, T, T), BF16),
            pltpu.VMEM((R, 2, F, RF), BF16),
            pltpu.VMEM((2, RF, RF), BF16),
            pltpu.VMEM((2, 2, F, RF), BF16),
            pltpu.VMEM((CHUNKS, R, F, CH), BF16),
            pltpu.VMEM((G, D, K, F, T), BF16),
            pltpu.VMEM((G, 2, D, K, F, T), BF16),
            pltpu.VMEM((G, BH, CF + KEEP, T), F32),
            pltpu.VMEM((G, S + 1, CF + KEEP, T), F32),
            pltpu.VMEM((BH, KEEP, T), F32),
            pltpu.VMEM((G, BH, CF, T), BF16),
            pltpu.VMEM((CHUNKS, RF, CH), F32),
            pltpu.VMEM((CHUNKS, RF, CH), BF16),
            pltpu.VMEM((CHUNKS, F, CH), BF16),
            pltpu.VMEM((CHUNKS, F, CH), F32),
            pltpu.VMEM((B, F, T), BF16),
            pltpu.VMEM((CHUNKS, CB, F, T), BF16),
            pltpu.VMEM((F, 2 * RF), F32),
            pltpu.VMEM((F, 2 * RF), F32),
            pltpu.VMEM((D, rows, 2 * RF), F32),
            pltpu.VMEM((D, rows, 2 * RF), F32),
            pltpu.VMEM((rows, 2 * RF), F32),
            pltpu.VMEM((D, K, F, T), BF16),
            pltpu.VMEM((L, B, F, T), F32),
            pltpu.SMEM((S,), jnp.int32),
            pltpu.SMEM((BH,), jnp.int32),
            dma((B,)),
            dma,
            dma((M,)),
            dma((2,)),
            dma((CHUNKS,)),
            dma((2,)),
            dma((G, PIECES)),
            dma((G, PIECES)),
            dma,
            dma,
            dma((G, PIECES)),
            dma((G, PIECES)),
            dma((G, D)),
            dma((G, D)),
            dma((G, D)),
            dma((G, D)),
            dma((R,)),
            dma((R,)),
            dma((CHUNKS,)),
            dma((CHUNKS,)),
            dma((G, 2, CHUNKS)),
            dma((G, 2, CHUNKS)),
            dma((CHUNKS,)),
            dma((CHUNKS,)),
            dma((CHUNKS,)),
            dma((CHUNKS,)),
            dma((CHUNKS,)),
            dma((CHUNKS,)),
            dma,
            dma,
            dma((D,)),
            dma((D,)),
            dma((D,)),
            dma((D,)),
            dma((D,)),
            dma((D,)),
        ],
        compiler_params=pltpu.CompilerParams(
            collective_id=0, has_side_effects=True, vmem_limit_bytes=limit
        ),
        name="layer_main",
    )(
        feats,
        w_self.T,
        w_neigh.T,
        local_cols.T,
        slist,
        rrows,
        local_tiles,
        far_tiles,
        cotangent,
    )
    output, grad_feats, gs, gn = pl.pallas_call(
        finish_kernel,
        out_shape=(
            jax.ShapeDtypeStruct((F, N), BF16),
            jax.ShapeDtypeStruct((F, N), BF16),
            jax.ShapeDtypeStruct((F, RF), F32),
            jax.ShapeDtypeStruct((F, RF), F32),
        ),
        in_specs=[smem, vmem, vmem, vmem, vmem],
        out_specs=(hbm, vmem, vmem, vmem),
        scratch_shapes=[pltpu.VMEM((F, N), F32), dma],
        compiler_params=pltpu.CompilerParams(vmem_limit_bytes=24 * 1024 * 1024),
        name="finish",
    )(slist, acc, back, final, output)
    return output, grad_feats, gs.T, gn.T


def solution(mesh):
    placed = (
        P("rep", "dom"),
        P(None, "rep"),
        P(None, "rep"),
        P("dom", None),
        P("dom", None, None, None),
        P("dom", None, None),
        P("dom", None, None),
        P("dom", None, None, None, None),
        P("rep", "dom"),
    )
    return jax.shard_map(
        functools.partial(local, mesh.shape["dom"], mesh.shape["rep"]),
        mesh=mesh,
        in_specs=placed,
        out_specs=(P("rep", "dom"), P("rep", "dom"), P(None, "rep"), P(None, "rep")),
        check_vma=False,
    )
```

```python
import functools

import jax
import jax.numpy as jnp
from jax import lax
from jax.experimental import pallas as pl
from jax.experimental.pallas import tpu as pltpu
from jax.sharding import PartitionSpec as P

MESH = pl.DeviceIdType.MESH
F32 = jnp.float32
BF16 = jnp.bfloat16
CHUNKS = 4
PIECES = 4
ONES = 16
KEEP = 8
NT = (((1,), (1,)), ((), ()))


def mm(a, b):
    return jnp.dot(a, b, preferred_element_type=F32)


def mm_nt(a, b):
    return lax.dot_general(a, b, NT, preferred_element_type=F32)


def equal_int(x, y):
    gap = x - y
    return 1 - jnp.minimum(gap * gap, 1)


def equal_one(x, y):
    return equal_int(x, y).astype(F32)


def rcopy(src, dst, send, recv, dom, rep):
    return pltpu.make_async_remote_copy(
        src_ref=src,
        dst_ref=dst,
        send_sem=send,
        recv_sem=recv,
        device_id={"dom": dom, "rep": rep},
        device_id_type=MESH,
    )


def main_kernel(
    D,
    R,
    feats_h,
    wts_h,
    wtn_h,
    cols,
    slist,
    rrows,
    ltiles_h,
    rtiles_h,
    cot_h,
    out_o,
    acc_o,
    back_o,
    final_o,
    fown,
    fmir,
    xchip,
    xmir,
    ltiles,
    rtiles,
    wall,
    wl,
    wb,
    cotb,
    hsend,
    hx,
    sums,
    chain,
    inv,
    xa,
    pre,
    gpb,
    outm,
    accm,
    scaled,
    scm,
    gown,
    gmate,
    gin,
    gw,
    gpart,
    red,
    ret,
    nearb,
    rowtab,
    prev,
    last,
    f_l,
    own_l,
    mir_l,
    w_l,
    c_l,
    t_l,
    xs_s,
    xs_r,
    xm_s,
    xm_r,
    xf_s,
    xf_r,
    h_s,
    h_r,
    hf_s,
    hf_r,
    w_s,
    w_r,
    cm_s,
    cm_r,
    cx_s,
    cx_r,
    om_s,
    om_r,
    am_s,
    am_r,
    sm_s,
    sm_r,
    gm_s,
    gm_r,
    b_s,
    b_r,
    p_s,
    p_r,
    f_s,
    f_r,
):
    d, r = lax.axis_index("dom"), lax.axis_index("rep")
    G = R // 2
    c, g = lax.rem(r, 2), lax.div(r, 2)
    mate = g * 2 + 1 - c
    F, N = feats_h.shape
    B, L, T, _ = ltiles.shape
    K = slist.shape[0]
    RF, CF, S = R * F, 2 * F, D * K
    BH, NH = B // 2, N // 2
    CB = BH // CHUNKS
    CH = CB * T
    PB = B // PIECES
    chips = [lax.rem(g + q, G) for q in range(G)]

    def peer(q, core):
        return chips[q] * 2 + core

    def ahead(p):
        return lax.rem(d + p, D)

    def half_cut(core, ch):
        return pl.ds(pl.multiple_of(core * NH + ch * CH, T), CH)

    def piece_cut(j):
        return pl.ds(j * PB, PB)

    def taken(ref, sem):
        pltpu.make_async_copy(ref, ref, sem).wait()

    def went(ref, sem):
        rcopy(ref, ref, sem, sem, d, mate).wait_send()

    def came(ref, sem):
        rcopy(ref, ref, sem, sem, d, mate).wait_recv()

    barrier = pltpu.get_barrier_semaphore()
    greeted = [(ahead(p), r) for p in range(1, D)] + [(d, mate)]
    greeted += [(d, peer(q, core)) for q in range(1, G) for core in range(2)]
    for dom, rep in greeted:
        pl.semaphore_signal(
            barrier, inc=1, device_id={"dom": dom, "rep": rep}, device_id_type=MESH
        )
    loads = [
        pltpu.make_async_copy(feats_h.at[:, b * T : (b + 1) * T], fown.at[b], f_l)
        for b in range(B)
    ]
    loads += [
        pltpu.make_async_copy(src, wall.at[r, i], w_l)
        for i, src in enumerate((wts_h, wtn_h))
    ]
    tile_loads = [
        pltpu.make_async_copy(ltiles_h, ltiles, t_l.at[0]),
        pltpu.make_async_copy(rtiles_h, rtiles, t_l.at[1]),
    ]
    loads += tile_loads
    loads += [
        pltpu.make_async_copy(cot_h.at[:, half_cut(c, ch)], cotb.at[ch, r], c_l)
        for ch in range(CHUNKS)
    ]
    for load in loads:
        load.start()
    taken(fown, f_l)
    pl.semaphore_wait(barrier, len(greeted))

    for j in range(PIECES):
        for q in range(1, G):
            rcopy(
                fown.at[piece_cut(j)],
                fmir.at[G - q - 1, piece_cut(j)],
                xs_s.at[q - 1],
                xs_r.at[G - q - 1, j],
                d,
                peer(q, c),
            ).start()
    mate_feat = rcopy(fown, xchip.at[c], xm_s, xm_r, d, mate)
    mate_feat.start()

    def send_halos(q, ref):
        def step(p, carry):
            to = ahead(p)
            for k in range(K):
                hsend[q, p, k] = ref(slist[k, to])
            rcopy(
                hsend.at[q, p], hx.at[q, c, p], h_s.at[q], h_r.at[q], to, r
            ).start()
            return carry

        lax.fori_loop(1, D, step, 0)

    others = pl.ds(1, D - 1)

    def halo_on(q):
        part = hx.at[q, c, others]
        return rcopy(part, part, hf_s.at[q], hf_r.at[q], d, mate)

    def pass_halo(q):
        came(hx.at[q, c, others], h_r.at[q])
        halo_on(q).start()

    send_halos(0, lambda block: fown[block])
    own_copy = pltpu.make_async_copy(fown, xchip.at[c], own_l)
    own_copy.start()
    taken(wall.at[r], w_l)
    weight_copies = [rcopy(wall.at[r], wall.at[r], w_s.at[0], w_r.at[0], d, mate)]
    for q in range(1, G):
        weight_copies.append(
            rcopy(wall.at[r], wall.at[r], w_s.at[q], w_r.at[q], d, peer(q, c))
        )
    for copy in weight_copies:
        copy.start()
    for ch in range(CHUNKS):
        for q in range(1, G):
            for core in range(2):
                rcopy(
                    cot_h.at[:, half_cut(core, ch)],
                    cotb.at[ch, r],
                    cx_s.at[q - 1],
                    cx_r.at[q - 1, ch],
                    d,
                    peer(q, core),
                ).start()
        rcopy(
            cot_h.at[:, half_cut(1 - c, ch)], cotb.at[ch, r], cm_s, cm_r, d, mate
        ).start()

    ones = jnp.ones((ONES, T), BF16)
    ones_wide = jnp.ones((ONES, L * T), BF16)

    def near(q, x):
        def step(i, carry):
            b = c * BH + i
            left = jnp.concatenate(
                [
                    jnp.concatenate([x(core, cols[l, b]) for core in range(2)], axis=0)
                    for l in range(L)
                ],
                axis=1,
            )
            if q == 0:
                left = jnp.concatenate([left, ones_wide], axis=0)
            right = jnp.concatenate([ltiles[b, l] for l in range(L)], axis=1)
            high = CF + KEEP if q == 0 else CF
            sums[q, i, :high] = mm_nt(left, right)[:high]
            return carry

        lax.fori_loop(0, BH, step, 0, unroll=4)

    def far(q):
        def step(p, carry):
            source = lax.rem(d - p + D, D)
            high = CF + KEEP if q == 0 else CF
            for k in range(K):
                s = p * K + k
                left = [hx[q, core, p, k] for core in range(2)]
                if q == 0:
                    left.append(ones)
                term = mm_nt(jnp.concatenate(left, axis=0), rtiles[source, k])[:high]
                chain[q, s + 1, :high] = term + chain[q, prev[s], :high]
            return carry

        lax.fori_loop(0, D, step, 0, unroll=4)

    def place(q):
        def step(i, carry):
            if q == 0:
                total = sums[q, i] + chain[q, last[i]]
                inverse = 1.0 / (1.0 + total[CF:])
                inv[i] = inverse
            else:
                total = sums[q, i, :CF] + chain[q, last[i], :CF]
                inverse = inv[i]
            xa[q, i] = (total[:CF] * inverse[:1]).astype(BF16)
            return carry

        lax.fori_loop(0, BH, step, 0, unroll=4)

    def pass_feats(j):
        for q in range(1, G):
            part = fmir.at[q - 1, piece_cut(j)]
            came(part, xs_r.at[q - 1, j])
            rcopy(
                part,
                xmir.at[q - 1, c, piece_cut(j)],
                xf_s.at[q - 1],
                xf_r.at[q - 1],
                d,
                mate,
            ).start()

    own_copy.wait()
    mate_feat.wait_recv()
    for k in range(K):
        for core in range(2):
            hx[0, core, 0, k] = xchip[core, slist[k, d]]
    tile_loads[0].wait()
    near(0, lambda core, col: xchip[core, col])
    tile_loads[1].wait()

    def list_rows(p, carry):
        source = lax.rem(d - p + D, D)
        for k in range(K):
            rowtab[p * K + k] = rrows[k, source]
        return carry

    lax.fori_loop(0, D, list_rows, 0)

    def previous(s, carry):
        row = rowtab[s]

        def look(j, found):
            before = jnp.minimum(jnp.maximum(s - j, 0), 1)
            return jnp.maximum(found, (j + 1) * before * equal_int(row, rowtab[j]))

        prev[s] = lax.fori_loop(0, S, look, 0, unroll=16)
        return carry

    lax.fori_loop(0, S, previous, 0)

    def latest(i, carry):
        def look(j, found):
            return jnp.maximum(found, (j + 1) * equal_int(c * BH + i, rowtab[j]))

        last[i] = lax.fori_loop(0, S, look, 0, unroll=16)
        return carry

    lax.fori_loop(0, BH, latest, 0)
    for q in range(G):
        chain[q, 0] = jnp.zeros((CF + KEEP, T), F32)
    pass_feats(0)
    pass_halo(0)
    for j in range(1, PIECES - 1):
        pass_feats(j)
    halo_on(0).wait_recv()
    far(0)
    place(0)
    pass_feats(PIECES - 1)
    for q in range(1, G):
        send_halos(q, lambda block: fmir[q - 1, block])
    mirror_copies = [
        pltpu.make_async_copy(fmir.at[q - 1], xmir.at[q - 1, c], mir_l.at[q - 1])
        for q in range(1, G)
    ]
    for copy in mirror_copies:
        copy.start()
    for q in range(1, G):
        t = lax.rem(g - q + G, G) * 2 + c
        weight_copies[q].wait_recv()
        slot = G + q - 1
        copy = rcopy(wall.at[t], wall.at[t], w_s.at[slot], w_r.at[slot], d, mate)
        copy.start()
        weight_copies.append(copy)
    weight_copies[0].wait_recv()
    for copy in weight_copies[G:]:
        copy.wait_recv()
    order = [r, mate] + [
        rep for q in range(1, G) for rep in (peer(q, c), peer(q, 1 - c))
    ]
    for i in range(2):
        for n, t in enumerate(order):
            for q in range(G):
                cut = pl.ds(pl.multiple_of(chips[q] * CF, CF), CF)
                wl[i, n * F : (n + 1) * F, q * CF : (q + 1) * CF] = wall[t, i, :, cut]
        turned = wl[i, :, :CF].astype(F32).T.astype(BF16)
        wb[i] = turned.reshape(2, F, RF)
    for copy in mirror_copies:
        copy.wait()
    for q in range(1, G):
        came(xmir.at[q - 1, 1 - c], xf_r.at[q - 1])
    for q in range(1, G):
        for k in range(K):
            for core in range(2):
                hx[q, core, 0, k] = xmir[q - 1, core, slist[k, d]]
        near(q, lambda core, col: xmir[q - 1, core, col])

    def stacked_x(ch):
        parts = []
        for i in range(CB):
            b = c * BH + ch * CB + i
            rows = [xchip[0, b], xchip[1, b]]
            for q in range(1, G):
                rows += [xmir[q - 1, 0, b], xmir[q - 1, 1, b]]
            parts.append(jnp.concatenate(rows, axis=0))
        return jnp.concatenate(parts, axis=1)

    def stacked_a(ch):
        return jnp.concatenate(
            [
                jnp.concatenate([xa[q, ch * CB + i] for q in range(G)], axis=0)
                for i in range(CB)
            ],
            axis=1,
        )

    for ch in range(CHUNKS):
        pre[ch] = mm(wl[0], stacked_x(ch))
    for q in range(1, G):
        pass_halo(q)
    for q in range(1, G):
        halo_on(q).wait_recv()
        far(q)
        place(q)

    taken(cotb.at[pl.ds(0, CHUNKS), r], c_l)
    came(cotb.at[pl.ds(0, CHUNKS), mate], cm_r)
    grads = jnp.zeros((CF, 2 * RF), F32)
    for ch in range(CHUNKS):
        cut = half_cut(c, ch)
        agg = stacked_a(ch)
        preact = pre[ch] + mm(wl[1], agg)
        s = jax.nn.sigmoid(preact)
        slope = s * (1.0 + preact * (1.0 - s))
        pre[ch, CF:] = slope[CF:]
        cot = jnp.concatenate([cotb[ch, t] for t in order[:2]], axis=0)
        gpb[ch, :CF] = (cot.astype(F32) * slope[:CF]).astype(BF16)
        result = (preact[:CF] * s[:CF]).astype(BF16)
        out_o[:, cut] = result[:F]
        outm[ch] = result[F:]
        rcopy(outm.at[ch], out_o.at[:, cut], om_s, om_r, d, mate).start()
        both = jnp.concatenate([stacked_x(ch), agg], axis=0)
        grads = grads + mm_nt(gpb[ch, :CF], both)
    gown[...] = grads[:F]
    gmate[...] = grads[F:]
    grad_copy = rcopy(gmate, gin, gm_s, gm_r, d, mate)
    grad_copy.start()
    back_left = jnp.concatenate([wb[0, c], wb[0, 1 - c], wb[1, c], wb[1, 1 - c]], axis=0)

    def back_chunk(ch):
        for q in range(1, G):
            t = lax.rem(g - q + G, G) * 2
            came(cotb.at[ch, pl.ds(t, 2)], cx_r.at[q - 1, ch])
        cut = half_cut(c, ch)
        cot = jnp.concatenate([cotb[ch, t] for t in order[2:]], axis=0)
        gpb[ch, CF:] = (cot.astype(F32) * pre[ch, CF:]).astype(BF16)
        back = mm(back_left, gpb[ch])
        at = pl.ds(c * BH + ch * CB, CB)
        for i in range(CB):
            lane = slice(i * T, (i + 1) * T)
            inverse = inv[ch * CB + i][:1]
            scaled[c * BH + ch * CB + i] = (back[CF : CF + F, lane] * inverse).astype(
                BF16
            )
            scm[ch, i] = (back[CF + F :, lane] * inverse).astype(BF16)
        rcopy(scm.at[ch], scaled.at[at], sm_s, sm_r, d, mate).start()
        acc_o[:, cut] = back[:F]
        accm[ch] = back[F:CF]
        rcopy(accm.at[ch], acc_o.at[:, cut], am_s, am_r, d, mate).start()

    rows = F // D
    for ch in range(CHUNKS):
        if ch == 1:
            grad_copy.wait_recv()
            own = gown[...] + gin[...]
            for p in range(D):
                for i in range(2):
                    for q in range(G):
                        to = pl.ds(pl.multiple_of(i * RF + chips[q] * CF, CF), CF)
                        lane = slice(i * RF + q * CF, i * RF + (q + 1) * CF)
                        gw[p, :, to] = own[p * rows : (p + 1) * rows, lane]

            def send_piece(p, carry):
                to = ahead(p)
                rcopy(gw.at[to], gpart.at[p], p_s, p_r, to, r).start()
                return carry

            lax.fori_loop(1, D, send_piece, 0)
        back_chunk(ch)

    came(scm, sm_r)

    def away(p, dst, slot):
        source = ahead(p)
        for k in range(K):
            block = scaled[rrows[k, source]]
            dst[slot, k] = mm(block, rtiles[source, k]).astype(BF16)

    def send_back(p, carry):
        away(p, ret, p)
        rcopy(ret.at[p], back_o.at[d], b_s, b_r, ahead(p), r).start()
        return carry

    lax.fori_loop(1, D, send_back, 0, unroll=7)
    away(0, back_o, d)

    came(gpart.at[others], p_r)

    def take_piece(p, total):
        return total + gpart[p]

    red[...] = lax.fori_loop(1, D, take_piece, gw[d])

    def send_final(p, carry):
        rcopy(red, final_o.at[d], f_s, f_r, ahead(p), r).start()
        return carry

    lax.fori_loop(1, D, send_final, 0)
    final_o[d] = red[...]

    def near_back(b, carry):
        right = jnp.concatenate([ltiles[b, l] for l in range(L)], axis=1)
        both = mm(scaled[b], right)
        for l in range(L):
            nearb[l, b] = both[:, l * T : (l + 1) * T]
        return carry

    lax.fori_loop(0, B, near_back, 0, unroll=4)
    came(accm, am_r)

    def gather_back(block, carry):
        at = pl.ds(pl.multiple_of(block * T, T), T)

        def add(i, total):
            for l in range(L):
                total = total + nearb[l, i] * equal_one(cols[l, i], block)
            return total

        acc_o[:, at] = lax.fori_loop(0, B, add, acc_o[:, at], unroll=8)
        return carry

    lax.fori_loop(0, B, gather_back, 0)

    came(ret.at[others], b_r)
    came(gpart.at[others], f_r)
    came(outm, om_r)
    went(ret.at[others], b_s)
    went(gpart.at[others], p_s)
    went(gpart.at[others], f_s)
    went(outm, om_s)
    went(accm, am_s)
    went(scm, sm_s)
    grad_copy.wait_send()
    went(cotb.at[pl.ds(0, CHUNKS), r], cm_s)
    mate_feat.wait_send()
    for q in range(1, G):
        went(fown, xs_s.at[q - 1])
        went(fown, xf_s.at[q - 1])
        went(cot_h, cx_s.at[q - 1])
    for q in range(G):
        went(hsend.at[q, others], h_s.at[q])
        halo_on(q).wait_send()
    for copy in weight_copies:
        copy.wait_send()


def finish_kernel(slist, acc, back, final, out_v, out_o, gf_o, gs_o, gn_o, total, sem):
    store = pltpu.make_async_copy(out_v, out_o, sem)
    store.start()
    total[...] = acc[...]
    D, K, _, T = back.shape
    _, rows, width = final.shape
    half = width // 2

    def home(s, carry):
        for k in range(K):
            at = pl.ds(pl.multiple_of(slist[k, s] * T, T), T)
            total[:, at] = total[:, at] + back[s, k].astype(F32)
        return carry

    lax.fori_loop(0, D, home, 0)
    gf_o[...] = total[...].astype(BF16)
    for p in range(D):
        part = final[p]
        where = slice(p * rows, (p + 1) * rows)
        gs_o[where, :] = part[:, :half]
        gn_o[where, :] = part[:, half:]
    store.wait()


def local(
    D,
    R,
    feats,
    w_self,
    w_neigh,
    local_cols,
    local_tiles,
    send_list,
    remote_rows,
    remote_tiles,
    cotangent,
):
    F, N = feats.shape
    B, L, T, _ = local_tiles.shape
    K = send_list.shape[2]
    G = R // 2
    RF, CF, S = R * F, 2 * F, D * K
    BH = B // 2
    CB = BH // CHUNKS
    CH = CB * T
    rows = F // D
    M = max(G - 1, 1)
    vmem = pl.BlockSpec(memory_space=pltpu.VMEM)
    smem = pl.BlockSpec(memory_space=pltpu.SMEM)
    hbm = pl.BlockSpec(memory_space=pltpu.HBM)
    dma = pltpu.SemaphoreType.DMA
    slist = jnp.swapaxes(send_list, 1, 2)[0]
    rrows = jnp.swapaxes(remote_rows, 1, 2)[0]
    far_tiles = remote_tiles[0]
    limit = 56 * 1024 * 1024
    output, acc, back, final = pl.pallas_call(
        functools.partial(main_kernel, D, R),
        out_shape=(
            pltpu.VMEM((F, N), BF16),
            pltpu.VMEM((F, N), F32),
            pltpu.VMEM((D, K, F, T), BF16),
            pltpu.VMEM((D, rows, 2 * RF), F32),
        ),
        in_specs=[hbm, hbm, hbm, smem, smem, smem, hbm, hbm, hbm],
        out_specs=(vmem, vmem, vmem, vmem),
        scratch_shapes=[
            pltpu.VMEM((B, F, T), BF16),
            pltpu.VMEM((M, B, F, T), BF16),
            pltpu.VMEM((2, B, F, T), BF16),
            pltpu.VMEM((M, 2, B, F, T), BF16),
            pltpu.VMEM((B, L, T, T), BF16),
            pltpu.VMEM((D, K, T, T), BF16),
            pltpu.VMEM((R, 2, F, RF), BF16),
            pltpu.VMEM((2, RF, RF), BF16),
            pltpu.VMEM((2, 2, F, RF), BF16),
            pltpu.VMEM((CHUNKS, R, F, CH), BF16),
            pltpu.VMEM((G, D, K, F, T), BF16),
            pltpu.VMEM((G, 2, D, K, F, T), BF16),
            pltpu.VMEM((G, BH, CF + KEEP, T), F32),
            pltpu.VMEM((G, S + 1, CF + KEEP, T), F32),
            pltpu.VMEM((BH, KEEP, T), F32),
            pltpu.VMEM((G, BH, CF, T), BF16),
            pltpu.VMEM((CHUNKS, RF, CH), F32),
            pltpu.VMEM((CHUNKS, RF, CH), BF16),
            pltpu.VMEM((CHUNKS, F, CH), BF16),
            pltpu.VMEM((CHUNKS, F, CH), F32),
            pltpu.VMEM((B, F, T), BF16),
            pltpu.VMEM((CHUNKS, CB, F, T), BF16),
            pltpu.VMEM((F, 2 * RF), F32),
            pltpu.VMEM((F, 2 * RF), F32),
            pltpu.VMEM((F, 2 * RF), F32),
            pltpu.VMEM((D, rows, 2 * RF), F32),
            pltpu.VMEM((D, rows, 2 * RF), F32),
            pltpu.VMEM((rows, 2 * RF), F32),
            pltpu.VMEM((D, K, F, T), BF16),
            pltpu.VMEM((L, B, F, T), F32),
            pltpu.SMEM((S,), jnp.int32),
            pltpu.SMEM((S,), jnp.int32),
            pltpu.SMEM((BH,), jnp.int32),
            dma,
            dma,
            dma((M,)),
            dma,
            dma,
            dma((2,)),
            dma((M,)),
            dma((M, PIECES)),
            dma,
            dma,
            dma((M,)),
            dma((M,)),
            dma((G,)),
            dma((G,)),
            dma((G,)),
            dma((G,)),
            dma((2 * G - 1,)),
            dma((2 * G - 1,)),
            dma,
            dma,
            dma((M,)),
            dma((M, CHUNKS)),
            dma,
            dma,
            dma,
            dma,
            dma,
            dma,
            dma,
            dma,
            dma,
            dma,
            dma,
            dma,
            dma,
            dma,
        ],
        compiler_params=pltpu.CompilerParams(
            collective_id=0, has_side_effects=True, vmem_limit_bytes=limit
        ),
        name="layer_main",
    )(
        feats,
        w_self.T,
        w_neigh.T,
        local_cols.T,
        slist,
        rrows,
        local_tiles,
        far_tiles,
        cotangent,
    )
    output, grad_feats, gs, gn = pl.pallas_call(
        finish_kernel,
        out_shape=(
            jax.ShapeDtypeStruct((F, N), BF16),
            jax.ShapeDtypeStruct((F, N), BF16),
            jax.ShapeDtypeStruct((F, RF), F32),
            jax.ShapeDtypeStruct((F, RF), F32),
        ),
        in_specs=[smem, vmem, vmem, vmem, vmem],
        out_specs=(hbm, vmem, vmem, vmem),
        scratch_shapes=[pltpu.VMEM((F, N), F32), dma],
        compiler_params=pltpu.CompilerParams(vmem_limit_bytes=24 * 1024 * 1024),
        name="finish",
    )(slist, acc, back, final, output)
    return output, grad_feats, gs.T, gn.T


def solution(mesh):
    placed = (
        P("rep", "dom"),
        P(None, "rep"),
        P(None, "rep"),
        P("dom", None),
        P("dom", None, None, None),
        P("dom", None, None),
        P("dom", None, None),
        P("dom", None, None, None, None),
        P("rep", "dom"),
    )
    return jax.shard_map(
        functools.partial(local, mesh.shape["dom"], mesh.shape["rep"]),
        mesh=mesh,
        in_specs=placed,
        out_specs=(P("rep", "dom"), P("rep", "dom"), P(None, "rep"), P(None, "rep")),
        check_vma=False,
    )
```

```python
import functools

import jax
import jax.numpy as jnp
from jax import lax
from jax.experimental import pallas as pl
from jax.experimental.pallas import tpu as pltpu
from jax.sharding import PartitionSpec as P

MESH = pl.DeviceIdType.MESH
F32 = jnp.float32
BF16 = jnp.bfloat16
CHUNKS = 4
PIECES = 4
ONES = 16
KEEP = 8
NT = (((1,), (1,)), ((), ()))


def mm(a, b):
    return jnp.dot(a, b, preferred_element_type=F32)


def mm_nt(a, b):
    return lax.dot_general(a, b, NT, preferred_element_type=F32)


def rcopy(src, dst, send, recv, dom, rep):
    return pltpu.make_async_remote_copy(
        src_ref=src,
        dst_ref=dst,
        send_sem=send,
        recv_sem=recv,
        device_id={"dom": dom, "rep": rep},
        device_id_type=MESH,
    )


def main_kernel(
    D,
    R,
    feats_h,
    wts_h,
    wtn_h,
    cols_h,
    slist_h,
    rrows_h,
    ltiles_h,
    rtiles_h,
    cot_h,
    out_o,
    gf_o,
    final_o,
    cols,
    slist,
    rrows,
    colv,
    slistv,
    rrowv,
    tabv,
    tab,
    acc,
    got,
    fown,
    fmir,
    xchip,
    xmir,
    ltiles,
    rtiles,
    wall,
    wl,
    wb,
    cotb,
    hsend,
    hx,
    sums,
    chain,
    inv,
    xa,
    pre,
    gpb,
    outm,
    accm,
    scaled,
    scm,
    gown,
    gmate,
    gin,
    gsum,
    gw,
    gpart,
    red,
    ret,
    nchain,
    hchain,
    i_l,
    tab_l,
    f_l,
    own_l,
    mir_l,
    w_l,
    c_l,
    t_l,
    xs_s,
    xs_r,
    xm_s,
    xm_r,
    xf_s,
    xf_r,
    h_s,
    h_r,
    hf_s,
    hf_r,
    w_s,
    w_r,
    cm_s,
    cm_r,
    cx_s,
    cx_r,
    om_s,
    om_r,
    am_s,
    am_r,
    sm_s,
    sm_r,
    gm_s,
    gm_r,
    b_s,
    b_r,
    p_s,
    p_r,
    f_s,
    f_r,
):
    d, r = lax.axis_index("dom"), lax.axis_index("rep")
    G = R // 2
    c, g = lax.rem(r, 2), lax.div(r, 2)
    mate = g * 2 + 1 - c
    F, N = feats_h.shape
    B, L, T, _ = ltiles.shape
    K = slist.shape[0]
    RF, CF = R * F, 2 * F
    BH, NH = B // 2, N // 2
    CB = BH // CHUNKS
    CH = CB * T
    PB = B // PIECES
    chips = [lax.rem(g + q, G) for q in range(G)]

    def peer(q, core):
        return chips[q] * 2 + core

    def ahead(p):
        return lax.rem(d + p, D)

    def half_cut(core, ch):
        return pl.ds(pl.multiple_of(core * NH + ch * CH, T), CH)

    def piece_cut(j):
        return pl.ds(j * PB, PB)

    def taken(ref, sem):
        pltpu.make_async_copy(ref, ref, sem).wait()

    def went(ref, sem):
        rcopy(ref, ref, sem, sem, d, mate).wait_send()

    def came(ref, sem):
        rcopy(ref, ref, sem, sem, d, mate).wait_recv()

    barrier = pltpu.get_barrier_semaphore()
    greeted = [(ahead(p), r) for p in range(1, D)] + [(d, mate)]
    greeted += [(d, peer(q, core)) for q in range(1, G) for core in range(2)]
    for dom, rep in greeted:
        pl.semaphore_signal(
            barrier, inc=1, device_id={"dom": dom, "rep": rep}, device_id_type=MESH
        )
    index_loads = [
        pltpu.make_async_copy(src, dst, i_l.at[i])
        for i, (src, dst) in enumerate(
            (
                (slist_h, slist),
                (rrows_h, rrows),
                (cols_h, cols),
                (cols_h, colv),
                (rrows_h, rrowv),
                (slist_h, slistv),
            )
        )
    ]
    loads = [
        pltpu.make_async_copy(feats_h.at[:, b * T : (b + 1) * T], fown.at[b], f_l)
        for b in range(B)
    ]
    loads += [
        pltpu.make_async_copy(src, wall.at[r, i], w_l)
        for i, src in enumerate((wts_h, wtn_h))
    ]
    tile_loads = [
        pltpu.make_async_copy(ltiles_h, ltiles, t_l.at[0]),
        pltpu.make_async_copy(rtiles_h, rtiles, t_l.at[1]),
    ]
    loads += tile_loads
    loads += [
        pltpu.make_async_copy(cot_h.at[:, half_cut(c, ch)], cotb.at[ch, r], c_l)
        for ch in range(CHUNKS)
    ]
    for load in index_loads + loads:
        load.start()
    pl.semaphore_wait(barrier, len(greeted))

    for j in range(PIECES):
        for q in range(1, G):
            for b in range(j * PB, (j + 1) * PB):
                rcopy(
                    feats_h.at[:, b * T : (b + 1) * T],
                    fmir.at[G - q - 1, b],
                    xs_s.at[q - 1],
                    xs_r.at[G - q - 1, j],
                    d,
                    peer(q, c),
                ).start()
    taken(fown, f_l)
    mate_feat = rcopy(fown, xchip.at[c], xm_s, xm_r, d, mate)
    mate_feat.start()

    def send_halos(q, ref):
        def step(p, carry):
            to = ahead(p)
            for k in range(K):
                hsend[q, p, k] = ref(slist[k, to])
            rcopy(
                hsend.at[q, p], hx.at[q, c, p], h_s.at[q], h_r.at[q, p], to, r
            ).start()
            return carry

        lax.fori_loop(1, D, step, 0)

    others = pl.ds(1, D - 1)

    def halo_on(q):
        part = hx.at[q, c, others]
        return rcopy(part, part, hf_s.at[q], hf_r.at[q], d, mate)

    def pass_halo(q):
        def step(p, carry):
            part = hx.at[q, c, p]
            came(part, h_r.at[q, p])
            rcopy(part, part, hf_s.at[q], hf_r.at[q], d, mate).start()
            return carry

        lax.fori_loop(1, D, step, 0)

    index_loads[0].wait()
    send_halos(0, lambda block: fown[block])
    own_copy = pltpu.make_async_copy(fown, xchip.at[c], own_l)
    own_copy.start()
    taken(wall.at[r], w_l)
    weight_copies = [rcopy(wall.at[r], wall.at[r], w_s.at[0], w_r.at[0], d, mate)]
    for q in range(1, G):
        weight_copies.append(
            rcopy(wall.at[r], wall.at[r], w_s.at[q], w_r.at[q], d, peer(q, c))
        )
    for copy in weight_copies:
        copy.start()
    for ch in range(CHUNKS):
        for q in range(1, G):
            for core in range(2):
                rcopy(
                    cot_h.at[:, half_cut(core, ch)],
                    cotb.at[ch, r],
                    cx_s.at[q - 1],
                    cx_r.at[q - 1, ch],
                    d,
                    peer(q, core),
                ).start()
        rcopy(
            cot_h.at[:, half_cut(1 - c, ch)], cotb.at[ch, r], cm_s, cm_r, d, mate
        ).start()

    ones = jnp.ones((ONES, T), BF16)
    ones_wide = jnp.ones((ONES, L * T), BF16)

    def near(q, x):
        def step(i, carry):
            b = c * BH + i
            left = jnp.concatenate(
                [
                    jnp.concatenate([x(core, cols[l, b]) for core in range(2)], axis=0)
                    for l in range(L)
                ],
                axis=1,
            )
            if q == 0:
                left = jnp.concatenate([left, ones_wide], axis=0)
            right = jnp.concatenate([ltiles[b, l] for l in range(L)], axis=1)
            high = CF + KEEP if q == 0 else CF
            sums[q, i, :high] = mm_nt(left, right)[:high]
            return carry

        lax.fori_loop(0, BH, step, 0, unroll=4)

    def far(q):
        def step(source, carry):
            p = lax.rem(d - source + D, D)
            high = CF + KEEP if q == 0 else CF
            for k in range(K):
                left = [hx[q, core, p, k] for core in range(2)]
                if q == 0:
                    left.append(ones)
                term = mm_nt(jnp.concatenate(left, axis=0), rtiles[source, k])[:high]
                before = tab[row_tab + 2 * k, source]
                chain[k, source + 1, :high] = term + chain[k, before, :high]
            return carry

        lax.fori_loop(0, D, step, 0, unroll=4)

    def place(q):
        def step(i, carry):
            high = CF + KEEP if q == 0 else CF
            total = sums[q, i, :high]
            for k in range(K):
                end = tab[row_tab + 2 * k + 1, c * BH + i]
                total = total + chain[k, end, :high]
            if q == 0:
                inverse = 1.0 / (1.0 + total[CF:])
                inv[i] = inverse
            else:
                inverse = inv[i]
            xa[q, i] = (total[:CF] * inverse[:1]).astype(BF16)
            return carry

        lax.fori_loop(0, BH, step, 0, unroll=4)

    def pass_feats(j):
        for q in range(1, G):
            part = fmir.at[q - 1, piece_cut(j)]
            came(part, xs_r.at[q - 1, j])
            rcopy(
                part,
                xmir.at[q - 1, c, piece_cut(j)],
                xf_s.at[q - 1],
                xf_r.at[q - 1],
                d,
                mate,
            ).start()

    for load in index_loads[1:]:
        load.wait()
    near_tab, row_tab, home_tab = 0, 2 * L, 2 * L + 2 * K

    def make_tables(first, ref, count):
        n = ref.shape[1]
        size = max(n, B)
        entry = lax.broadcasted_iota(jnp.int32, (n, size), 0)
        place_of = lax.broadcasted_iota(jnp.int32, (n, size), 1)
        for i in range(count):
            across = jnp.broadcast_to(ref[i : i + 1, :], (n, n))
            down = across.astype(F32).T.astype(jnp.int32)
            older = (across == down) & (entry[:, :n] < place_of[:, :n])
            before = jnp.max(jnp.where(older, entry[:, :n] + 1, 0), axis=0)
            wide = jnp.broadcast_to(down[:, :1], (n, size))
            end = jnp.max(jnp.where(wide == place_of, entry + 1, 0), axis=0)
            tabv[first + 2 * i, :n] = before
            tabv[first + 2 * i + 1, :size] = end

    make_tables(near_tab, colv, L)
    make_tables(row_tab, rrowv, K)
    make_tables(home_tab, slistv, K)
    tab_copy = pltpu.make_async_copy(tabv, tab, tab_l)
    tab_copy.start()
    chain[:, 0] = jnp.zeros((K, CF + KEEP, T), F32)
    nchain[:, 0] = jnp.zeros((L, F, T), F32)
    hchain[:, 0] = jnp.zeros((K, F, T), F32)
    own_copy.wait()
    mate_feat.wait_recv()
    for k in range(K):
        for core in range(2):
            hx[0, core, 0, k] = xchip[core, slist[k, d]]
    tile_loads[0].wait()
    near(0, lambda core, col: xchip[core, col])
    tile_loads[1].wait()

    tab_copy.wait()
    pass_feats(0)
    pass_halo(0)
    for j in range(1, PIECES - 1):
        pass_feats(j)
    halo_on(0).wait_recv()
    far(0)
    place(0)
    pass_feats(PIECES - 1)
    for q in range(1, G):
        send_halos(q, lambda block: fmir[q - 1, block])
    mirror_copies = [
        pltpu.make_async_copy(fmir.at[q - 1], xmir.at[q - 1, c], mir_l.at[q - 1])
        for q in range(1, G)
    ]
    for copy in mirror_copies:
        copy.start()
    for q in range(1, G):
        t = lax.rem(g - q + G, G) * 2 + c
        weight_copies[q].wait_recv()
        slot = G + q - 1
        copy = rcopy(wall.at[t], wall.at[t], w_s.at[slot], w_r.at[slot], d, mate)
        copy.start()
        weight_copies.append(copy)
    weight_copies[0].wait_recv()
    for copy in weight_copies[G:]:
        copy.wait_recv()
    order = [r, mate] + [
        rep for q in range(1, G) for rep in (peer(q, c), peer(q, 1 - c))
    ]
    for i in range(2):
        for n, t in enumerate(order):
            for q in range(G):
                cut = pl.ds(pl.multiple_of(chips[q] * CF, CF), CF)
                wl[i, n * F : (n + 1) * F, q * CF : (q + 1) * CF] = wall[t, i, :, cut]
        turned = wl[i, :, :CF].astype(F32).T.astype(BF16)
        wb[i] = turned.reshape(2, F, RF)
    for copy in mirror_copies:
        copy.wait()
    for q in range(1, G):
        came(xmir.at[q - 1, 1 - c], xf_r.at[q - 1])
    for q in range(1, G):
        for k in range(K):
            for core in range(2):
                hx[q, core, 0, k] = xmir[q - 1, core, slist[k, d]]
        near(q, lambda core, col: xmir[q - 1, core, col])

    def stacked_x(ch):
        parts = []
        for i in range(CB):
            b = c * BH + ch * CB + i
            rows = [xchip[0, b], xchip[1, b]]
            for q in range(1, G):
                rows += [xmir[q - 1, 0, b], xmir[q - 1, 1, b]]
            parts.append(jnp.concatenate(rows, axis=0))
        return jnp.concatenate(parts, axis=1)

    def stacked_a(ch):
        return jnp.concatenate(
            [
                jnp.concatenate([xa[q, ch * CB + i] for q in range(G)], axis=0)
                for i in range(CB)
            ],
            axis=1,
        )

    for ch in range(CHUNKS):
        pre[ch] = mm(wl[0], stacked_x(ch))
    for q in range(1, G):
        pass_halo(q)
    for q in range(1, G):
        halo_on(q).wait_recv()
        far(q)
        place(q)

    taken(cotb.at[pl.ds(0, CHUNKS), r], c_l)
    came(cotb.at[pl.ds(0, CHUNKS), mate], cm_r)
    grads = jnp.zeros((CF, 2 * RF), F32)
    for ch in range(CHUNKS):
        cut = half_cut(c, ch)
        agg = stacked_a(ch)
        preact = pre[ch] + mm(wl[1], agg)
        s = jax.nn.sigmoid(preact)
        slope = s * (1.0 + preact * (1.0 - s))
        pre[ch, CF:] = slope[CF:]
        cot = jnp.concatenate([cotb[ch, t] for t in order[:2]], axis=0)
        gpb[ch, :CF] = (cot.astype(F32) * slope[:CF]).astype(BF16)
        result = (preact[:CF] * s[:CF]).astype(BF16)
        out_o[:, cut] = result[:F]
        outm[ch] = result[F:]
        rcopy(outm.at[ch], out_o.at[:, cut], om_s, om_r, d, mate).start()
        both = jnp.concatenate([stacked_x(ch), agg], axis=0)
        grads = grads + mm_nt(gpb[ch, :CF], both)
    gown[...] = grads[:F]
    gmate[...] = grads[F:]
    grad_copy = rcopy(gmate, gin, gm_s, gm_r, d, mate)
    grad_copy.start()
    back_left = jnp.concatenate([wb[0, c], wb[0, 1 - c], wb[1, c], wb[1, 1 - c]], axis=0)

    def back_chunk(ch):
        for q in range(1, G):
            t = lax.rem(g - q + G, G) * 2
            came(cotb.at[ch, pl.ds(t, 2)], cx_r.at[q - 1, ch])
        cut = half_cut(c, ch)
        cot = jnp.concatenate([cotb[ch, t] for t in order[2:]], axis=0)
        gpb[ch, CF:] = (cot.astype(F32) * pre[ch, CF:]).astype(BF16)
        back = mm(back_left, gpb[ch])
        at = pl.ds(c * BH + ch * CB, CB)
        for i in range(CB):
            lane = slice(i * T, (i + 1) * T)
            inverse = inv[ch * CB + i][:1]
            scaled[c * BH + ch * CB + i] = (back[CF : CF + F, lane] * inverse).astype(
                BF16
            )
            scm[ch, i] = (back[CF + F :, lane] * inverse).astype(BF16)
        rcopy(scm.at[ch], scaled.at[at], sm_s, sm_r, d, mate).start()
        acc[:, cut] = back[:F]
        accm[ch] = back[F:CF]
        rcopy(accm.at[ch], acc.at[:, cut], am_s, am_r, d, mate).start()

    rows = F // D
    for ch in range(CHUNKS):
        if ch == CHUNKS - 1:
            grad_copy.wait_recv()
            own = gown[...] + gin[...]
            for p in range(D):
                for i in range(2):
                    for q in range(G):
                        to = pl.ds(pl.multiple_of(i * RF + chips[q] * CF, CF), CF)
                        lane = slice(i * RF + q * CF, i * RF + (q + 1) * CF)
                        gsum[p, :, to] = own[p * rows : (p + 1) * rows, lane]
                gw[p] = gsum[p].astype(BF16)

            def send_piece(p, carry):
                to = ahead(p)
                rcopy(gw.at[to], gpart.at[p], p_s, p_r, to, r).start()
                return carry

            lax.fori_loop(1, D, send_piece, 0)
        back_chunk(ch)

    came(scm, sm_r)

    def away(p, dst, slot):
        source = ahead(p)
        for k in range(K):
            block = scaled[rrows[k, source]]
            dst[slot, k] = mm(block, rtiles[source, k]).astype(BF16)

    def send_back(p, carry):
        away(p, ret, p)
        rcopy(ret.at[p], got.at[d], b_s, b_r, ahead(p), r).start()
        return carry

    early = (D + 1) // 2
    lax.fori_loop(1, early, send_back, 0, unroll=3)

    came(gpart.at[others], p_r)

    def take_piece(p, total):
        return total + gpart[p].astype(F32)

    red[...] = lax.fori_loop(1, D, take_piece, gsum[d]).astype(BF16)

    def send_final(p, carry):
        rcopy(red, final_o.at[d], f_s, f_r, ahead(p), r).start()
        return carry

    lax.fori_loop(1, D, send_final, 0)
    final_o[d] = red[...]
    lax.fori_loop(early, D, send_back, 0, unroll=4)
    away(0, got, d)

    def near_back(b, carry):
        right = jnp.concatenate([ltiles[b, l] for l in range(L)], axis=1)
        both = mm(scaled[b], right)
        for l in range(L):
            before = tab[near_tab + 2 * l, b]
            nchain[l, b + 1] = both[:, l * T : (l + 1) * T] + nchain[l, before]
        return carry

    lax.fori_loop(0, B, near_back, 0, unroll=4)
    came(accm, am_r)

    def gather_near(block, carry):
        at = pl.ds(pl.multiple_of(block * T, T), T)
        total = acc[:, at]
        for l in range(L):
            total = total + nchain[l, tab[near_tab + 2 * l + 1, block]]
        acc[:, at] = total
        return carry

    lax.fori_loop(0, B, gather_near, 0, unroll=4)

    came(ret.at[others], b_r)
    def home(s, carry):
        for k in range(K):
            before = tab[home_tab + 2 * k, s]
            hchain[k, s + 1] = got[s, k].astype(F32) + hchain[k, before]
        return carry

    lax.fori_loop(0, D, home, 0, unroll=4)

    def gather_home(block, carry):
        at = pl.ds(pl.multiple_of(block * T, T), T)
        total = acc[:, at]
        for k in range(K):
            total = total + hchain[k, tab[home_tab + 2 * k + 1, block]]
        gf_o[:, at] = total.astype(BF16)
        return carry

    lax.fori_loop(0, B, gather_home, 0, unroll=4)

    came(gpart.at[others], f_r)
    came(outm, om_r)
    went(ret.at[others], b_s)
    went(gpart.at[others], p_s)
    went(gpart.at[others], f_s)
    went(outm, om_s)
    went(accm, am_s)
    went(scm, sm_s)
    grad_copy.wait_send()
    went(cotb.at[pl.ds(0, CHUNKS), r], cm_s)
    mate_feat.wait_send()
    for q in range(1, G):
        went(fown, xs_s.at[q - 1])
        went(fown, xf_s.at[q - 1])
        went(cot_h, cx_s.at[q - 1])
    for q in range(G):
        went(hsend.at[q, others], h_s.at[q])
        halo_on(q).wait_send()
    for copy in weight_copies:
        copy.wait_send()


def finish_kernel(final, out_v, gf_v, out_o, gf_o, gs_o, gn_o, sem):
    stores = [
        pltpu.make_async_copy(src, dst, sem.at[i])
        for i, (src, dst) in enumerate(((out_v, out_o), (gf_v, gf_o)))
    ]
    for store in stores:
        store.start()
    half = gs_o.shape[2]
    gs_o[...] = final[:, :, :half].astype(F32)
    gn_o[...] = final[:, :, half:].astype(F32)
    for store in stores:
        store.wait()


def local(
    D,
    R,
    feats,
    w_self,
    w_neigh,
    local_cols,
    local_tiles,
    send_list,
    remote_rows,
    remote_tiles,
    cotangent,
):
    F, N = feats.shape
    B, L, T, _ = local_tiles.shape
    K = send_list.shape[2]
    G = R // 2
    RF, CF = R * F, 2 * F
    BH = B // 2
    CB = BH // CHUNKS
    CH = CB * T
    rows = F // D
    M = max(G - 1, 1)
    tables = -(-(2 * L + 4 * K) // 8) * 8
    vmem = pl.BlockSpec(memory_space=pltpu.VMEM)
    hbm = pl.BlockSpec(memory_space=pltpu.HBM)
    dma = pltpu.SemaphoreType.DMA
    slist = jnp.swapaxes(send_list, 1, 2)[0]
    rrows = jnp.swapaxes(remote_rows, 1, 2)[0]
    far_tiles = remote_tiles[0]
    limit = 56 * 1024 * 1024
    output, grad_feats, final = pl.pallas_call(
        functools.partial(main_kernel, D, R),
        out_shape=(
            pltpu.VMEM((F, N), BF16),
            pltpu.VMEM((F, N), BF16),
            pltpu.VMEM((D, rows, 2 * RF), BF16),
        ),
        in_specs=[hbm] * 9,
        out_specs=(vmem, vmem, vmem),
        scratch_shapes=[
            pltpu.SMEM((L, B), jnp.int32),
            pltpu.SMEM((K, D), jnp.int32),
            pltpu.SMEM((K, D), jnp.int32),
            pltpu.VMEM((L, B), jnp.int32),
            pltpu.VMEM((K, D), jnp.int32),
            pltpu.VMEM((K, D), jnp.int32),
            pltpu.VMEM((tables, T), jnp.int32),
            pltpu.SMEM((tables, T), jnp.int32),
            pltpu.VMEM((F, N), F32),
            pltpu.VMEM((D, K, F, T), BF16),
            pltpu.VMEM((B, F, T), BF16),
            pltpu.VMEM((M, B, F, T), BF16),
            pltpu.VMEM((2, B, F, T), BF16),
            pltpu.VMEM((M, 2, B, F, T), BF16),
            pltpu.VMEM((B, L, T, T), BF16),
            pltpu.VMEM((D, K, T, T), BF16),
            pltpu.VMEM((R, 2, F, RF), BF16),
            pltpu.VMEM((2, RF, RF), BF16),
            pltpu.VMEM((2, 2, F, RF), BF16),
            pltpu.VMEM((CHUNKS, R, F, CH), BF16),
            pltpu.VMEM((G, D, K, F, T), BF16),
            pltpu.VMEM((G, 2, D, K, F, T), BF16),
            pltpu.VMEM((G, BH, CF + KEEP, T), F32),
            pltpu.VMEM((K, D + 1, CF + KEEP, T), F32),
            pltpu.VMEM((BH, KEEP, T), F32),
            pltpu.VMEM((G, BH, CF, T), BF16),
            pltpu.VMEM((CHUNKS, RF, CH), F32),
            pltpu.VMEM((CHUNKS, RF, CH), BF16),
            pltpu.VMEM((CHUNKS, F, CH), BF16),
            pltpu.VMEM((CHUNKS, F, CH), F32),
            pltpu.VMEM((B, F, T), BF16),
            pltpu.VMEM((CHUNKS, CB, F, T), BF16),
            pltpu.VMEM((F, 2 * RF), F32),
            pltpu.VMEM((F, 2 * RF), F32),
            pltpu.VMEM((F, 2 * RF), F32),
            pltpu.VMEM((D, rows, 2 * RF), F32),
            pltpu.VMEM((D, rows, 2 * RF), BF16),
            pltpu.VMEM((D, rows, 2 * RF), BF16),
            pltpu.VMEM((rows, 2 * RF), BF16),
            pltpu.VMEM((D, K, F, T), BF16),
            pltpu.VMEM((L, B + 1, F, T), F32),
            pltpu.VMEM((K, D + 1, F, T), F32),
            dma((6,)),
            dma,
            dma,
            dma,
            dma((M,)),
            dma,
            dma,
            dma((2,)),
            dma((M,)),
            dma((M, PIECES)),
            dma,
            dma,
            dma((M,)),
            dma((M,)),
            dma((G,)),
            dma((G, D)),
            dma((G,)),
            dma((G,)),
            dma((2 * G - 1,)),
            dma((2 * G - 1,)),
            dma,
            dma,
            dma((M,)),
            dma((M, CHUNKS)),
            dma,
            dma,
            dma,
            dma,
            dma,
            dma,
            dma,
            dma,
            dma,
            dma,
            dma,
            dma,
            dma,
            dma,
        ],
        compiler_params=pltpu.CompilerParams(
            collective_id=0, has_side_effects=True, vmem_limit_bytes=limit
        ),
        name="layer_main",
    )(
        feats,
        w_self.T,
        w_neigh.T,
        local_cols.T,
        slist,
        rrows,
        local_tiles,
        far_tiles,
        cotangent,
    )
    output, grad_feats, gs, gn = pl.pallas_call(
        finish_kernel,
        out_shape=(
            jax.ShapeDtypeStruct((F, N), BF16),
            jax.ShapeDtypeStruct((F, N), BF16),
            jax.ShapeDtypeStruct((D, rows, RF), F32),
            jax.ShapeDtypeStruct((D, rows, RF), F32),
        ),
        in_specs=[vmem, vmem, vmem],
        out_specs=(hbm, hbm, vmem, vmem),
        scratch_shapes=[dma((2,))],
        compiler_params=pltpu.CompilerParams(vmem_limit_bytes=24 * 1024 * 1024),
        name="finish",
    )(final, output, grad_feats)
    return output, grad_feats, gs.reshape(F, RF).T, gn.reshape(F, RF).T


def solution(mesh):
    placed = (
        P("rep", "dom"),
        P(None, "rep"),
        P(None, "rep"),
        P("dom", None),
        P("dom", None, None, None),
        P("dom", None, None),
        P("dom", None, None),
        P("dom", None, None, None, None),
        P("rep", "dom"),
    )
    return jax.shard_map(
        functools.partial(local, mesh.shape["dom"], mesh.shape["rep"]),
        mesh=mesh,
        in_specs=placed,
        out_specs=(P("rep", "dom"), P("rep", "dom"), P(None, "rep"), P(None, "rep")),
        check_vma=False,
    )
```
